32 devices in a mesh: grp: 2 (over y), scen: 4 (over z), blk: 2 (over x), sub: 2 (over core).
Axes of the slice: x: 2, y: 2, z: 4, core: 2. Of those that a mesh axis runs over, the one named last changes fastest.
Arguments:
- block_matrices: float32 [8, 256, 128, 128], P(('grp', 'scen'), ('blk', 'sub')), parts along dimension 0, may hold values from -0.25 to 0.25
- slot_row_block: int32 [8, 256], P(('grp', 'scen'), ('blk', 'sub')), parts along dimension 0, may hold values from 0 to 7
- tile_column: int32 [8, 256], P(('grp', 'scen'), ('blk', 'sub')), parts along dimension 0, may hold values from 0 to 4127, as said below
- block_count: int32 [8, 4], P(('grp', 'scen'), ('blk', 'sub')), parts along dimension 0, may hold values from 8 to 64, as said below
- carbon_scenario: int32 [8], P(('grp', 'scen')), parts along dimension 0, may hold values from 0 to 23
- intensity: float32 [24, 32, 128], P(None, ('blk', 'sub')), may hold values from 0.2 to 2
- cost_first: float32 [8192, 128], P(('grp', 'scen', 'blk', 'sub')), parts along dimension 0, may hold values from -6 to 6
- lower_first: float32 [8192, 128], P(('grp', 'scen', 'blk', 'sub')), parts along dimension 0, may hold values from -1 to -0.2
- upper_first: float32 [8192, 128], P(('grp', 'scen', 'blk', 'sub')), parts along dimension 0, may hold values from 0.2 to 1
- cost_second: float32 [8, 32, 128], P(('grp', 'scen'), ('blk', 'sub')), parts along dimension 0, may hold values from -6 to 6
- upper_second: float32 [8, 32, 128], P(('grp', 'scen'), ('blk', 'sub')), parts along dimension 0, may hold values from 0.2 to 2
- row_bound: float32 [8, 32, 128], P(('grp', 'scen'), ('blk', 'sub')), parts along dimension 0, may hold values from -20 to 20
- first_start: float32 [8192, 128], P(('grp', 'scen', 'blk', 'sub')), parts along dimension 0, may hold values from -0.2 to 0.2
- second_start: float32 [8, 32, 128], P(('grp', 'scen'), ('blk', 'sub')), parts along dimension 0, may hold values from 0 to 0.2
- dual_start: float32 [8, 32, 128], P(('grp', 'scen'), ('blk', 'sub')), parts along dimension 0, may hold values from 0 to 1
Outputs:
- first_final: float32 [8192, 128], P(('grp', 'scen', 'blk', 'sub')), parts along dimension 0
- second_final: float32 [8, 32, 128], P(('grp', 'scen'), ('blk', 'sub')), parts along dimension 0
- dual_final: float32 [8, 32, 128], P(('grp', 'scen'), ('blk', 'sub')), parts along dimension 0
- residual_norm: float32 [6], P('grp'), parts along dimension 0
The draws below stay inside these ranges and needn't reach their ends.
There are 2 independent parts, one for each index of `grp`. The reference program is written for one: setup_inputs(seed, part) draws one part's arguments, and reference() takes and returns one part's arrays. A program takes and returns all parts, laid end to end along the dimension named above; an argument that names none is the same for every part. Nothing has to cross between parts.
Inputs may be any that keep to these rules, and one draw needn't show every extreme that they name: `block_count`: each scenario has one index of blk and sub with all 64 slots used; the others use between 8 and 32. `tile_column`: values below 4096 name first-section column blocks, values from 4096 on second-section ones. Split the first-section blocks into 16 equal shards in order, and take the slots of one index of scen and of blk and sub together (64 of them, scenario by scenario). In every draw, on every such device, at most 4 of them name first-section blocks of one shard, and some shard is named by exactly 4.
All inputs are finite; a program needn't handle non-finite values.
Results may differ from the reference program's by a relative error of at most 0.0003.
Values sent between devices are 32-bit elements; how exact they have to be, the bound alone decides.
No kernel may reach another device: no remote copies, remote signals or barrier semaphores. Data moves between devices by JAX's collectives and lax.ppermute only.
A program may use at most 64 MiB of HBM per device.

```python
import math
import jax
import jax.numpy as jnp
from jax import lax

BLOCK_EXTENT = 128
NB1 = 4096
S_DEV = 1
ROW_BLOCKS_LOCAL = 8
NCARB = 24
ITERS = 3
KCAP = 64
GROUPS = 4
SCENARIO_COUNT = 4
MB = 32
NB2 = 32
SLOT_COUNT = 256


def draw_tile_column(key, part):
    key_pick, key_first, key_second, key_shift = jax.random.split(key, 4)
    array_shape = (SCENARIO_COUNT, SLOT_COUNT)
    owner_count = SCENARIO_COUNT // S_DEV * GROUPS
    shard_width = NB1 // owner_count
    scen_index = jnp.arange(SCENARIO_COUNT, dtype=jnp.int32)[:, None]
    index_of_slot = jnp.arange(SLOT_COUNT, dtype=jnp.int32)[None, :]
    device = scen_index // S_DEV * GROUPS + index_of_slot // KCAP
    position = scen_index % S_DEV * KCAP + index_of_slot % KCAP
    shifts = jax.random.randint(key_shift, (owner_count,), 0, owner_count)
    owner = (position + shifts[device]) % owner_count
    first_index = owner * shard_width + jax.random.randint(key_first, array_shape, 0, shard_width)
    pick = jax.random.randint(key_pick, array_shape, 0, 2)
    pick = jnp.where(position % owner_count == 0, 0, pick)
    second_index = jax.random.randint(key_second, array_shape, 0, NB2)
    column = jnp.where(pick == 0, first_index, NB1 + second_index).astype(jnp.int32)
    column = column.at[0, 1].set(NB1 + NB2 - 1)
    return column.astype(jnp.int32)


def draw_block_count(key, part):
    key_base, key_full = jax.random.split(key, 2)
    base = jax.random.randint(key_base, (SCENARIO_COUNT, GROUPS), KCAP // 8, KCAP // 2 + 1)
    full = jax.random.randint(key_full, (SCENARIO_COUNT, 1), 0, GROUPS)
    position = jnp.arange(GROUPS, dtype=jnp.int32)[None, :]
    return jnp.where(position == full, KCAP, base).astype(jnp.int32)


def draw_row_bound(key, part):
    key_value, key_scale = jax.random.split(key, 2)
    array_shape = (SCENARIO_COUNT, MB, BLOCK_EXTENT)
    scales = jnp.exp(jax.random.uniform(key_scale, array_shape, jnp.float32, 0.0, math.log(10.0))) / 3.0
    values = jnp.clip(jax.random.normal(key_value, array_shape, jnp.float32), -6.0, 6.0)
    return (values * scales).astype(jnp.float32)


def plant(values, stream_key, smallest, largest):
    longest = values.shape.index(max(values.shape))
    spots = []
    for shift in (0, 1):
        where = [jax.random.randint(jax.random.fold_in(stream_key, axis), (), 0, length) for axis, length in enumerate(values.shape)]
        where[longest] = (where[longest] + shift) % values.shape[longest]
        spots.append(tuple(where))
    return values.at[spots[0]].set(smallest).at[spots[1]].set(largest)


def levels(rng, dims, cuts, smallest, top_value):
    def one(dim, blocks):
        steps = jax.random.uniform(jax.random.fold_in(jax.random.fold_in(rng, 6), dim), (blocks,), jnp.float32, smallest / len(cuts), top_value / len(cuts))
        return jnp.repeat(jnp.exp(steps), dims[dim] // blocks).reshape((-1,) + (1,) * (len(dims) - dim - 1))

    level = one(*cuts[0])
    for cut in cuts[1:]:
        level = level * one(*cut)
    return level


def gaussian(key, shape, scale, most, cuts=(), kind=jnp.bfloat16):
    level = levels(key, shape, cuts, -0.22, 0.18) if cuts else 1.0
    array = jax.random.normal(key, shape, jnp.float32) * scale * level
    return jnp.minimum(jnp.maximum(array, -most), most).astype(kind)


def setup_inputs(seed: int = 0, part: int = 0) -> dict:
    keys = jax.random.split(jax.random.key(seed), 16)
    own_keys = jax.random.split(jax.random.fold_in(keys[15], part), 16)
    return {
        "block_matrices": gaussian(own_keys[0], (SCENARIO_COUNT, SLOT_COUNT, BLOCK_EXTENT, BLOCK_EXTENT), (4 * BLOCK_EXTENT) ** -0.5, 0.25, ((0, 4), (1, 4)), jnp.float32),
        "slot_row_block": plant(jax.random.randint(own_keys[1], (SCENARIO_COUNT, SLOT_COUNT), 0, ROW_BLOCKS_LOCAL), jax.random.fold_in(own_keys[1], 1), 0, ROW_BLOCKS_LOCAL - 1).astype(jnp.int32),
        "tile_column": draw_tile_column(jax.random.fold_in(jax.random.fold_in(keys[15], part), 71), part),
        "block_count": draw_block_count(jax.random.fold_in(jax.random.fold_in(keys[15], part), 71), part),
        "carbon_scenario": plant(jax.random.randint(own_keys[4], (SCENARIO_COUNT,), 0, NCARB), jax.random.fold_in(own_keys[4], 1), 0, NCARB - 1).astype(jnp.int32),
        "intensity": jnp.clip(jnp.exp(math.log(2.0) - 2.3025851 * jax.random.uniform(keys[5], (NCARB, NB2, BLOCK_EXTENT), jnp.float32) ** levels(keys[5], (NCARB, NB2, BLOCK_EXTENT), ((1, 4),), -0.2, 0.2)), 0.2, 2.0),
        "cost_first": gaussian(own_keys[6], (NB1, BLOCK_EXTENT), 1.0, 6.0, ((0, 16),), jnp.float32),
        "lower_first": jnp.clip(-1.0 + 0.8 * jax.random.uniform(own_keys[7], (NB1, BLOCK_EXTENT), jnp.float32) ** levels(own_keys[7], (NB1, BLOCK_EXTENT), ((0, 16),), -0.2, 0.2), -1.0, -0.2),
        "upper_first": jnp.clip(0.2 + 0.8 * jax.random.uniform(own_keys[8], (NB1, BLOCK_EXTENT), jnp.float32) ** levels(own_keys[8], (NB1, BLOCK_EXTENT), ((0, 16),), -0.2, 0.2), 0.2, 1.0),
        "cost_second": gaussian(own_keys[9], (SCENARIO_COUNT, NB2, BLOCK_EXTENT), 1.0, 6.0, ((0, 4), (1, 4)), jnp.float32),
        "upper_second": jnp.clip(0.2 + 1.8 * jax.random.uniform(own_keys[10], (SCENARIO_COUNT, NB2, BLOCK_EXTENT), jnp.float32) ** levels(own_keys[10], (SCENARIO_COUNT, NB2, BLOCK_EXTENT), ((0, 4), (1, 4)), -0.2, 0.2), 0.2, 2.0),
        "row_bound": draw_row_bound(jax.random.fold_in(jax.random.fold_in(keys[15], part), 71), part),
        "first_start": jnp.clip(jax.random.uniform(own_keys[12], (NB1, BLOCK_EXTENT), jnp.float32, -0.2, 0.2) * levels(own_keys[12], (NB1, BLOCK_EXTENT), ((0, 16),), -0.4, 0.0), -0.2, 0.2),
        "second_start": jnp.clip(0.2 * jax.random.uniform(own_keys[13], (SCENARIO_COUNT, NB2, BLOCK_EXTENT), jnp.float32) ** levels(own_keys[13], (SCENARIO_COUNT, NB2, BLOCK_EXTENT), ((0, 4), (1, 4)), -0.2, 0.2), 0.0, 0.2),
        "dual_start": jnp.clip(1.0 * jax.random.uniform(own_keys[14], (SCENARIO_COUNT, MB, BLOCK_EXTENT), jnp.float32) ** levels(own_keys[14], (SCENARIO_COUNT, MB, BLOCK_EXTENT), ((0, 4), (1, 4)), -0.2, 0.2), 0.0, 1.0),
    }


precise = lax.Precision.HIGHEST
step_primal = 0.4
step_dual = 0.4

def reference(block_matrices, slot_row_block, tile_column, block_count, carbon_scenario, intensity, cost_first, lower_first, upper_first, cost_second, upper_second, row_bound, first_start, second_start, dual_start):
    slots = slot_row_block.shape[1]
    groups = block_count.shape[1]
    kcap = slots // groups
    rows_total = row_bound.shape[1]
    rows_group = rows_total // groups
    tile_size = row_bound.shape[2]
    count_first = cost_first.shape[0]
    count_second = cost_second.shape[1]
    index_of_slot = jnp.arange(slots, dtype=jnp.int32)
    group_of = (index_of_slot // kcap).astype(jnp.int32)
    limit = jnp.take(block_count, group_of, axis=1)
    mask = ((index_of_slot % kcap)[None, :] < limit).astype(jnp.float32)
    row_global = (group_of[None, :] * rows_group + slot_row_block).astype(jnp.int32)
    cost_total = cost_second + intensity[carbon_scenario]

    def adjoint(dual):

        def one_scenario(args):
            tile_one, rows_one, columns_one, mask_one, dual_one = args
            product = jnp.einsum('kij,ki->kj', tile_one, dual_one[rows_one], precision=precise) * mask_one[:, None]
            is_first = columns_one < count_first
            first_index = jnp.where(is_first, columns_one, count_first).astype(jnp.int32)
            second_index = jnp.where(is_first, count_second, columns_one - count_first).astype(jnp.int32)
            first_terms = jnp.zeros((count_first, tile_size), jnp.float32).at[first_index].add(product, mode='drop')
            second_terms = jnp.zeros((count_second, tile_size), jnp.float32).at[second_index].add(product, mode='drop')
            return (first_terms, second_terms)
        first_all, second_all = lax.map(one_scenario, (block_matrices, row_global, tile_column, mask, dual))
        return (lax.optimization_barrier(jnp.sum(first_all, axis=0)), second_all)

    def forward(first_bar, second_bar):

        def one_scenario(args):
            tile_one, rows_one, columns_one, mask_one, second_one = args
            is_first = columns_one < count_first
            from_first = first_bar[jnp.clip(columns_one, 0, count_first - 1).astype(jnp.int32)]
            from_second = second_one[jnp.clip(columns_one - count_first, 0, count_second - 1).astype(jnp.int32)]
            blocks = jnp.where(is_first[:, None], from_first, from_second)
            product = jnp.einsum('kij,kj->ki', tile_one, blocks, precision=precise) * mask_one[:, None]
            return jnp.zeros((rows_total, tile_size), jnp.float32).at[rows_one].add(product)
        return lax.map(one_scenario, (block_matrices, row_global, tile_column, mask, second_bar))
    first_now = first_start
    second_now = second_start
    dual = dual_start
    norms = []
    for step_index in range(ITERS):
        grad_first, grad_second = adjoint(dual)
        first_next = jnp.clip(first_now - step_primal * (cost_first - grad_first), lower_first, upper_first)
        second_next = jnp.clip(second_now - step_primal * (cost_total - grad_second), 0.0, upper_second)
        first_bar = 2.0 * first_next - first_now
        second_bar = 2.0 * second_next - second_now
        residual = row_bound - forward(first_bar, second_bar)
        norms.append(jnp.sqrt(jnp.sum(residual * residual) / residual.size))
        dual = jnp.maximum(dual + step_dual * residual, 0.0)
        first_now = first_next
        second_now = second_next
    return (first_now, second_now, dual, jnp.stack(norms))
```

```python
import functools

import jax
import jax.numpy as jnp
from jax import lax
from jax.experimental import pallas as pl
from jax.experimental.pallas import tpu as pltpu
from jax.sharding import PartitionSpec as P

ITERS = 3
STEP_PRIMAL = 0.4
STEP_DUAL = 0.4
SHARED = 4
GROUP = ("scen", "blk", "sub")
PAIR = ("blk", "sub")
F32 = jnp.float32
VM = pl.BlockSpec(memory_space=pltpu.VMEM)
SM = pl.BlockSpec(memory_space=pltpu.SMEM)
ACCS = 2


def exact_dot(a, b, contract=(1, 0)):
    dims = (((contract[0],), (contract[1],)), ((), ()))
    return lax.dot_general(a, b, dims, precision=lax.Precision.HIGHEST, preferred_element_type=F32)


def count_dot(a, b):
    return jnp.dot(a, b, preferred_element_type=F32)


def iota(shape, dim):
    return lax.broadcasted_iota(jnp.int32, shape, dim).astype(F32)


def as_float(flags):
    return jnp.where(flags, 1.0, 0.0).astype(F32)


def earlier(size):
    return as_float(iota((size, size), 0) < iota((size, size), 1))


def second_onehot(ids_row, count_first, count_second):
    slots = ids_row.shape[1]
    return as_float(ids_row - float(count_first) == iota((count_second, slots), 0))


def adjoint_products(blocks, rows, spread, parts):
    slots, tile, _ = blocks.shape
    for n in range(slots):
        row = rows[0, n]
        total = None
        for i in range(tile // 8):
            term = blocks[n, pl.ds(i * 8, 8), :] * spread[row, pl.ds(i * 8, 8), :]
            total = term if total is None else total + term
        parts[n] = total
    return jnp.sum(parts[...], axis=1)


def spread_duals(dual_t, spread):
    tile = spread.shape[1]
    for r in range(spread.shape[0]):
        spread[r] = jnp.broadcast_to(dual_t[:, r : r + 1], (tile, tile))


def start_kernel(sizes, blocks, rows, ids, dual, bound, cost2, upper2, second, intensity, carbon,
                 prod_out, sec_out, dual_out, bound_out, spread, parts, square):
    tile, own2, count_first, count_second = sizes
    local_rows = dual.shape[0]
    for source, target in ((dual, dual_out), (bound, bound_out)):
        square[...] = jnp.zeros_like(square)
        square[pl.ds(0, local_rows), :] = source[...]
        target[...] = jnp.transpose(square[...])
    spread_duals(dual_out[...], spread)
    prod = adjoint_products(blocks, rows, spread, parts)
    prod_out[...] = prod
    onehot = second_onehot(ids[...].astype(F32), count_first, count_second)
    sec_out[pl.ds(0, count_second), :] = exact_dot(onehot, prod)
    sec_out[pl.ds(count_second, own2), :] = cost2[...] + intensity[carbon[0]]
    sec_out[pl.ds(count_second + own2, own2), :] = upper2[...]
    sec_out[pl.ds(count_second + 2 * own2, own2), :] = second[...]


def plan_kernel(sizes, everyone, ids, prod, cost, lower, upper, first,
                send_out, pick_out, own_out, sum_out, square, shared):
    devices, slots, shard, count_first, most, keep, me_axes = sizes
    me = lax.axis_index(me_axes).astype(F32)
    base = me * float(shard)
    table = everyone[:, 0, :].astype(F32)
    row = ids[...].astype(F32)
    before = earlier(slots)
    asked = as_float((table >= base) & (table < base + float(shard)))
    rank = count_dot(asked, before)
    slot_number = iota((devices, slots), 1)
    lane = iota((devices, 128), 1)
    id_row = jnp.full((devices, 128), -1.0, F32)
    places = []
    for q in range(most):
        chosen = asked * as_float(rank == float(q))
        has = jnp.sum(chosen, axis=1, keepdims=True)
        place = jnp.sum(chosen * (table - base), axis=1, keepdims=True)
        number = jnp.sum(chosen * slot_number, axis=1, keepdims=True)
        places.append(jnp.where(has > 0.0, place, -1.0))
        id_row = jnp.where(lane == float(q), jnp.where(has > 0.0, number, -1.0), id_row)
    wanted = as_float(jnp.concatenate(places, axis=0) == iota((most * devices, shard), 1))
    for a, source in enumerate((cost, lower, upper, first)):
        answer = exact_dot(wanted, source[...])
        for q in range(most):
            send_out[:, q * 4 + a, :] = answer[q * devices : (q + 1) * devices]
    eye = as_float(iota((slots, slots), 0) == iota((slots, slots), 1))
    column = jnp.sum(eye * row, axis=1, keepdims=True)
    own = as_float(column == row)
    own_out[...] = own
    total = exact_dot(own, prod[...])
    sum_out[...] = total
    again = jnp.max(own * before, axis=0, keepdims=True)
    usable = as_float((row >= 0.0) & (row < float(count_first))) * (1.0 - again)
    square[...] = jnp.full_like(square, -5.0)
    square[pl.ds(0, devices), pl.ds(0, slots)] = table
    turned = jnp.transpose(square[...])
    for e in range(devices):
        named = as_float(turned[:slots, e : e + 1] == row)
        shared[pl.ds(e, 1), :] = jnp.max(named, axis=0, keepdims=True) * usable
    both = shared[...] * as_float(iota((devices, slots), 0) != me)
    count = jnp.max(jnp.sum(both, axis=1, keepdims=True), axis=0, keepdims=True)
    id_row = jnp.where(lane == float(most + keep), as_float(count > float(keep)), id_row)
    rank = count_dot(both, before)
    picks = []
    for p in range(keep):
        chosen = both * as_float(rank == float(p))
        has = jnp.sum(chosen, axis=1, keepdims=True)
        name = jnp.sum(chosen * row, axis=1, keepdims=True)
        id_row = jnp.where(lane == float(most + p), jnp.where(has > 0.0, name, -1.0), id_row)
        picks.append(chosen)
    pick = jnp.concatenate(picks, axis=0)
    pick_out[...] = pick
    rows = exact_dot(pick, total)
    for p in range(keep):
        send_out[:, most * 4 + p, :] = rows[p * devices : (p + 1) * devices]
    send_out[:, most * 4 + keep, :] = id_row


def side_kernel(sizes, everyone, ids, cost, lower, upper, first, base_out, place_out, reply_out):
    devices, slots, shard, most, me_axes = sizes
    base = lax.axis_index(me_axes).astype(F32) * float(shard)
    table = everyone[:, 0, :].astype(F32)
    row = ids[...].astype(F32)
    before = earlier(slots)
    asked = as_float((table >= base) & (table < base + float(shard)))
    rank = count_dot(asked, before)
    places = []
    for q in range(most):
        chosen = asked * as_float(rank == float(q))
        has = jnp.sum(chosen, axis=1, keepdims=True)
        place = jnp.sum(chosen * (table - base), axis=1, keepdims=True)
        places.append(jnp.where(has > 0.0, place, -1.0))
    wanted = as_float(jnp.concatenate(places, axis=0) == iota((most * devices, shard), 1))
    below = as_float(iota((most * devices, most * devices), 0) > iota((most * devices, most * devices), 1))
    wanted = wanted * as_float(count_dot(below, wanted) == 0.0)
    place_out[...] = wanted
    touched = exact_dot(wanted, jnp.ones((most * devices, cost.shape[1]), F32), (0, 0))
    x = first[...]
    for _ in range(ITERS):
        x = jnp.clip(x - STEP_PRIMAL * cost[...], lower[...], upper[...])
    base_out[...] = jnp.where(touched > 0.0, 0.0, x)
    owner = iota((devices, slots), 0) * float(shard)
    held = as_float((row >= owner) & (row < owner + float(shard)))
    rank = count_dot(held, before)
    for q in range(most):
        reply_out[pl.ds(q * devices, devices), :] = held * as_float(rank == float(q))


def step_kernel(sizes, first_step, last_step, direct, *refs):
    devices, slots, count_first, count_second, own2, peers, most, keep, cells = sizes
    refs = list(refs)
    take = lambda: refs.pop(0)
    blocks, rows, ids, dual_t, bound_t = take(), take(), take(), take(), take()
    row = ids[...].astype(F32)
    if first_step:
        answer = take()
        own_sum = None if direct else take()
        gradient = take() if direct else None
        sec_own = take()
        sec_in = [take() for _ in range(len(peers))]
    else:
        x_in, cost_in, lower_in, upper_in, match_in = take(), take(), take(), take(), take()
        y_in, cost2_in, upper2_in = take(), take(), take()
        if direct:
            gradient = take()
        else:
            own_sum, received = take(), take()
        sec_own = take()
        sec_in = [take() for _ in range(len(peers))]
    if not last_step:
        if not direct:
            own_in, pick_in = take(), take()
    else:
        reply_in = take()
        squares_in = [take() for _ in range(ITERS - 1)]
    if first_step:
        cost_out, lower_out, upper_out, match_out, cost2_out, upper2_out = [take() for _ in range(6)]
    if last_step:
        reply_out, y_out, dual_out = take(), take(), take()
    else:
        x_out, y_out, dual_out, square_out, sec_out, sum_out = [take() for _ in range(6)]
        send_out = None if direct else take()
    spread, parts, second_all = take(), take(), take()
    accs = [take() for _ in range(ACCS)]
    square = take()

    if first_step:
        me2 = lax.axis_index(PAIR)
        for k, source in [(0, sec_own)] + list(zip(peers, sec_in)):
            place = pl.multiple_of(lax.bitwise_xor(me2, k) * own2, own2)
            for a in range(3):
                second_all[a, pl.ds(place, own2), :] = source[pl.ds(count_second + a * own2, own2), :]
        cost2, upper2, y = second_all[0], second_all[1], second_all[2]
        cost2_out[...] = cost2
        upper2_out[...] = upper2
        id_row = answer[:, most * 4 + keep, :]
        names = jnp.concatenate([id_row[:, q : q + 1] for q in range(most)], axis=0)
        place = as_float(names == iota((most * devices, slots), 1))
        got = []
        for a in range(4):
            stacked = jnp.concatenate([answer[:, q * 4 + a, :] for q in range(most)], axis=0)
            got.append(exact_dot(place, stacked, (0, 0)))
        cost, lower, upper, x = got
        cost_out[...] = cost
        lower_out[...] = lower
        upper_out[...] = upper
        names = jnp.concatenate([id_row[:, most + p : most + p + 1] for p in range(keep)], axis=0)
        match = as_float(names == row)
        match_out[...] = match
        if not direct:
            fresh = jnp.concatenate([answer[:, most * 4 + p, :] for p in range(keep)], axis=0)
    else:
        x, cost, lower, upper, match = x_in[...], cost_in[...], lower_in[...], upper_in[...], match_in[...]
        y, cost2, upper2 = y_in[...], cost2_in[...], upper2_in[...]
        if not direct:
            fresh = jnp.concatenate([received[:, p, :] for p in range(keep)], axis=0)
    if direct:
        grad = gradient[...]
    else:
        grad = own_sum[...] + exact_dot(match, fresh, (0, 0))
    grad2 = sec_own[pl.ds(0, count_second), :]
    for source in sec_in:
        grad2 = grad2 + source[pl.ds(0, count_second), :]
    x_next = jnp.clip(x - STEP_PRIMAL * (cost - grad), lower, upper)
    y_next = jnp.clip(y - STEP_PRIMAL * (cost2 - grad2), 0.0, upper2)
    onehot = second_onehot(row, count_first, count_second)
    parts[0:slots // 8] = (
        (2.0 * x_next - x) + exact_dot(onehot, 2.0 * y_next - y, (0, 0))
    ).reshape(slots // 8, 8, x.shape[1])
    y_out[...] = y_next
    for acc in accs:
        acc[...] = jnp.zeros_like(acc)
    tile = blocks.shape[1]
    bars = parts[0:slots // 8].reshape(slots, tile)
    for n in range(slots):
        r = rows[0, n]
        acc = accs[n % ACCS]
        bar = jnp.broadcast_to(bars[n : n + 1, :], (8, tile))
        for i in range(tile // 8):
            acc[r, pl.ds(i * 8, 8), :] += blocks[n, pl.ds(i * 8, 8), :] * bar
    local_rows = spread.shape[0]
    duals = dual_t[...]
    bounds = bound_t[...]
    lane = lax.broadcasted_iota(jnp.int32, (tile, tile), 1)
    next_dual = jnp.zeros((tile, tile), F32)
    squares = jnp.zeros((tile, 1), F32)
    for r in range(local_rows):
        total = accs[0][r]
        for acc in accs[1:]:
            total = total + acc[r]
        residual = bounds[:, r : r + 1] - jnp.sum(total, axis=1, keepdims=True)
        squares = squares + residual * residual
        column = jnp.maximum(duals[:, r : r + 1] + STEP_DUAL * residual, 0.0)
        wide = jnp.broadcast_to(column, (tile, tile))
        spread[r] = wide
        next_dual = jnp.where(lane == r, wide, next_dual)
    squares = jnp.broadcast_to(jnp.sum(squares, axis=0, keepdims=True), (1, tile))
    if last_step:
        square[...] = jnp.transpose(next_dual)
        dual_out[...] = square[pl.ds(0, local_rows), :]
        lanes = lax.broadcasted_iota(jnp.int32, (1, tile), 1)
        note = jnp.zeros((1, tile), F32)
        for k, value in enumerate([s[...] for s in squares_in] + [squares]):
            note = jnp.where(lanes == k, value, note)
        reply = exact_dot(reply_in[...], x_next)
        for q in range(most):
            reply_out[:, q, :] = reply[q * devices : (q + 1) * devices]
        reply_out[:, most, :] = jnp.broadcast_to(note, (devices, tile))
    else:
        x_out[...] = x_next
        dual_out[...] = next_dual
        square_out[...] = squares
        prod = adjoint_products(blocks, rows, spread, parts)
        sec_out[...] = exact_dot(onehot, prod)
        if direct:
            sum_out[...] = prod
        else:
            total = exact_dot(own_in[...], prod)
            sum_out[...] = total
            out = exact_dot(pick_in[...], total)
            for p in range(keep):
                send_out[:, p, :] = out[p * devices : (p + 1) * devices]


def finish_kernel(sizes, reply, base, place, first_out, norm_out):
    devices, most, cells = sizes
    rows = jnp.concatenate([reply[:, q, :] for q in range(most)], axis=0)
    first_out[...] = base[...] + exact_dot(place[...], rows, (0, 0))
    norm_out[...] = jnp.sqrt(jnp.sum(reply[:, most, :], axis=0, keepdims=True) / float(cells))


def shards(
    block_matrices,
    slot_row_block,
    tile_column,
    block_count,
    carbon_scenario,
    intensity,
    cost_first,
    lower_first,
    upper_first,
    cost_second,
    upper_second,
    row_bound,
    first_start,
    second_start,
    dual_start,
):
    devices = lax.axis_size(GROUP)
    pairs = lax.axis_size(PAIR)
    scenarios, slots = slot_row_block.shape
    local_rows, tile = row_bound.shape[1:]
    shard = cost_first.shape[0]
    own2 = cost_second.shape[1]
    count_first = shard * devices
    count_second = own2 * pairs
    cells = scenarios * local_rows * tile * devices
    most = -(-scenarios * slots // devices)
    keep = SHARED
    peers = list(range(1, pairs))

    def shape(*dims):
        return jax.ShapeDtypeStruct(dims, F32)

    def scratch(*dims):
        return pltpu.VMEM(dims, F32)

    params = pltpu.CompilerParams(vmem_limit_bytes=40 << 20)

    blocks = block_matrices[0]
    used = jnp.arange(slots, dtype=jnp.int32)[None, :] < block_count
    ids = jnp.where(used, tile_column, -1)
    everyone = lax.all_to_all(
        jnp.broadcast_to(ids[None], (devices, 1, slots)), GROUP, 0, 0, tiled=True
    )
    prod, sec, dual_t, bound_t = pl.pallas_call(
        functools.partial(start_kernel, (tile, own2, count_first, count_second)),
        out_shape=(shape(slots, tile), shape(count_second + 3 * own2, tile), shape(tile, tile), shape(tile, tile)),
        in_specs=[VM, SM, VM, VM, VM, VM, VM, VM, VM, SM],
        scratch_shapes=[scratch(local_rows, tile, tile), scratch(slots, 8, tile), scratch(tile, tile)],
        compiler_params=params,
        name="start",
    )(blocks, slot_row_block, ids, dual_start[0], row_bound[0], cost_second[0], upper_second[0],
      second_start[0], intensity, carbon_scenario)
    firsts = (cost_first, lower_first, upper_first, first_start)
    width = -(-(most * 4 + keep + 1) // 8) * 8
    send, pick, own, own_sum = pl.pallas_call(
        functools.partial(plan_kernel, (devices, slots, shard, count_first, most, keep, GROUP)),
        out_shape=(shape(devices, width, tile), shape(keep * devices, slots), shape(slots, slots), shape(slots, tile)),
        in_specs=[VM] * 7,
        scratch_shapes=[scratch(128, 128), scratch(devices, slots)],
        compiler_params=params,
        name="plan",
    )(everyone, ids, prod, *firsts)
    answer = lax.all_to_all(send, GROUP, 0, 0, tiled=True)
    base, place, reply_pick = pl.pallas_call(
        functools.partial(side_kernel, (devices, slots, shard, most, GROUP)),
        out_shape=(shape(shard, tile), shape(most * devices, shard), shape(most * devices, slots)),
        in_specs=[VM] * 6,
        compiler_params=params,
        name="side",
    )(everyone, ids, *firsts)

    def swap(value):
        return [lax.ppermute(value, PAIR, [(i, i ^ k) for i in range(pairs)]) for k in peers]

    sec_in = swap(sec)
    overflow = jnp.max(answer[:, most * 4 + keep, most + keep]) > 0.5
    step_sizes = (devices, slots, count_first, count_second, own2, peers, most, keep, cells)
    step_scratch = (
        [scratch(local_rows, tile, tile), scratch(slots, 8, tile), scratch(3, count_second, tile)]
        + [scratch(local_rows, tile, tile)] * ACCS
        + [scratch(tile, tile)]
    )
    reply_width = -(-(most + 1) // 8) * 8

    def exchange(value):
        gathered = lax.all_gather(value, GROUP, axis=0, tiled=True)
        match = (everyone.reshape(1, -1) == ids.reshape(-1, 1)).astype(F32)
        return jnp.dot(match, gathered, precision=lax.Precision.HIGHEST)

    def iterate(direct, operands):
        answer, prod, own_sum, sec, dual_t, sec_in = operands
        squares = []
        for step in range(ITERS):
            first_step, last_step = step == 0, step == ITERS - 1
            args = [blocks, slot_row_block, ids, dual_t, bound_t]
            if first_step:
                args.append(answer)
                args.append(exchange(prod) if direct else own_sum)
            else:
                args += [x, cost, lower, upper, match, y, cost2, upper2]
                args += [exchange(own_sum)] if direct else [own_sum, lax.all_to_all(send, GROUP, 0, 0, tiled=True)]
                sec_in = swap(sec)
            args += [sec] + list(sec_in)
            if last_step:
                args += [reply_pick] + squares
                outs = [shape(devices, reply_width, tile), shape(count_second, tile), shape(local_rows, tile)]
            else:
                if not direct:
                    args += [own, pick]
                outs = [shape(slots, tile), shape(count_second, tile), shape(tile, tile), shape(1, tile),
                        shape(count_second, tile), shape(slots, tile)]
                if not direct:
                    outs.append(shape(devices, keep, tile))
            if first_step:
                outs = [shape(slots, tile)] * 3 + [shape(keep * devices, slots)] + [shape(count_second, tile)] * 2 + outs
            results = list(
                pl.pallas_call(
                    functools.partial(step_kernel, step_sizes, first_step, last_step, direct),
                    out_shape=tuple(outs),
                    in_specs=[VM, SM] + [VM] * (len(args) - 2),
                    scratch_shapes=step_scratch,
                    compiler_params=params,
                    name="step",
                )(*args)
            )
            if first_step:
                cost, lower, upper, match, cost2, upper2 = results[:6]
                results = results[6:]
            if last_step:
                reply, y, dual = results
            else:
                x, y, dual_t, square, sec, own_sum = results[:6]
                squares.append(square)
                if not direct:
                    send = results[6]
        return lax.all_to_all(reply, GROUP, 0, 0, tiled=True), y, dual

    reply, y, dual = lax.cond(
        overflow,
        functools.partial(iterate, True),
        functools.partial(iterate, False),
        (answer, prod, own_sum, sec, dual_t, sec_in),
    )
    first_final, norms = pl.pallas_call(
        functools.partial(finish_kernel, (devices, most, cells)),
        out_shape=(shape(shard, tile), shape(1, tile)),
        in_specs=[VM] * 3,
        compiler_params=params,
        name="finish",
    )(reply, base, place)
    second_final = lax.dynamic_slice_in_dim(y, lax.axis_index(PAIR) * own2, own2, 0)
    return first_final, second_final[None], dual[None], norms[0, :ITERS]


def solution(mesh):
    return jax.shard_map(
        shards,
        mesh=mesh,
        in_specs=(
            P(("grp", "scen"), ("blk", "sub"), None, None),
            P(("grp", "scen"), ("blk", "sub")),
            P(("grp", "scen"), ("blk", "sub")),
            P(("grp", "scen"), ("blk", "sub")),
            P(("grp", "scen")),
            P(None, ("blk", "sub"), None),
            P(("grp", "scen", "blk", "sub"), None),
            P(("grp", "scen", "blk", "sub"), None),
            P(("grp", "scen", "blk", "sub"), None),
            P(("grp", "scen"), ("blk", "sub"), None),
            P(("grp", "scen"), ("blk", "sub"), None),
            P(("grp", "scen"), ("blk", "sub"), None),
            P(("grp", "scen", "blk", "sub"), None),
            P(("grp", "scen"), ("blk", "sub"), None),
            P(("grp", "scen"), ("blk", "sub"), None),
        ),
        out_specs=(
            P(("grp", "scen", "blk", "sub"), None),
            P(("grp", "scen"), ("blk", "sub"), None),
            P(("grp", "scen"), ("blk", "sub"), None),
            P("grp"),
        ),
        check_vma=False,
    )
```

```python
import functools

import jax
import jax.numpy as jnp
from jax import lax
from jax.experimental import pallas as pl
from jax.experimental.pallas import tpu as pltpu
from jax.sharding import PartitionSpec as P

ITERS = 3
STEP_PRIMAL = 0.4
STEP_DUAL = 0.4
SHARED = 4
GROUP = ("scen", "blk", "sub")
PAIR = ("blk", "sub")
F32 = jnp.float32
VM = pl.BlockSpec(memory_space=pltpu.VMEM)
SM = pl.BlockSpec(memory_space=pltpu.SMEM)
HB = pl.BlockSpec(memory_space=pl.ANY)
ACCS = 2
CHUNK = 16


def exact_dot(a, b, contract=(1, 0)):
    dims = (((contract[0],), (contract[1],)), ((), ()))
    return lax.dot_general(a, b, dims, precision=lax.Precision.HIGHEST, preferred_element_type=F32)


def count_dot(a, b):
    return jnp.dot(a, b, preferred_element_type=F32)


def iota(shape, dim):
    return lax.broadcasted_iota(jnp.int32, shape, dim).astype(F32)


def as_float(flags):
    return jnp.where(flags, 1.0, 0.0).astype(F32)


def earlier(size):
    return as_float(iota((size, size), 0) < iota((size, size), 1))


def second_onehot(ids_row, count_first, count_second):
    slots = ids_row.shape[1]
    return as_float(ids_row - float(count_first) == iota((count_second, slots), 0))


def fetch_blocks(source, target, sems):
    copies = [
        pltpu.make_async_copy(source.at[pl.ds(k, CHUNK)], target.at[pl.ds(k, CHUNK)], sems.at[k // CHUNK])
        for k in range(0, target.shape[0], CHUNK)
    ]
    for copy in copies:
        copy.start()

    def wait(n):
        if n % CHUNK == 0:
            copies[n // CHUNK].wait()

    return wait


def adjoint_products(kept, rows, spread, parts):
    slots, tile, _ = kept.shape
    for n in range(slots):
        row = rows[0, n]
        total = None
        for i in range(tile // 16):
            part = pl.ds(i * 16, 16)
            term = kept[n, part, :].astype(F32) * spread[row, part, :]
            total = term if total is None else total + term
        parts[n] = total[:8] + total[8:]
    return jnp.sum(parts[...], axis=1)


def spread_duals(dual_t, spread):
    tile = spread.shape[1]
    for r in range(spread.shape[0]):
        spread[r] = jnp.broadcast_to(dual_t[:, r : r + 1], (tile, tile))


def start_kernel(sizes, blocks_in, rows, used, columns, dual, bound, cost2, upper2, second, intensity, carbon,
                 ids_out, prod_out, sec_out, dual_out, bound_out, own_out, sum_out, usable_out,
                 spread, parts, squares, prices, blocks, sems, block_sems):
    tile, own2, count_first, count_second = sizes
    slots = blocks.shape[0]
    local_rows = dual.shape[0]
    places = [sec_out.at[pl.ds(count_second + a * own2, own2), :] for a in range(3)]
    copies = [
        pltpu.make_async_copy(source, target, sems.at[k])
        for k, (source, target) in enumerate([
            (dual, squares.at[0, pl.ds(0, local_rows), :]),
            (bound, squares.at[1, pl.ds(0, local_rows), :]),
            (cost2, places[0]),
            (upper2, places[1]),
            (second, places[2]),
            (intensity.at[carbon[0]], prices),
        ])
    ]
    for copy in copies:
        copy.start()
    wait = fetch_blocks(blocks_in, blocks, block_sems)
    row = columns[...].astype(F32)
    ids_out[...] = row
    active = as_float(iota((slots, tile), 0) < used[0, 0].astype(F32))
    eye = as_float(iota((slots, slots), 0) == iota((slots, slots), 1))
    column = jnp.sum(eye * row, axis=1, keepdims=True)
    own = as_float(column == row)
    own_out[...] = own
    again = jnp.max(own * earlier(slots), axis=0, keepdims=True)
    some = jnp.max(own * active[:, :1], axis=0, keepdims=True)
    usable_out[...] = as_float(row < float(count_first)) * (1.0 - again) * some
    for k in range(2):
        squares[k, pl.ds(local_rows, tile - local_rows), :] = jnp.zeros((tile - local_rows, tile), F32)
    for copy in copies:
        copy.wait()
    for k, target in enumerate((dual_out, bound_out)):
        target[...] = jnp.transpose(squares[k])
    spread_duals(dual_out[...], spread)
    for n in range(slots):
        wait(n)
        r = rows[0, n]
        total = None
        for i in range(tile // 8):
            term = blocks[n, pl.ds(i * 8, 8), :] * spread[r, pl.ds(i * 8, 8), :]
            total = term if total is None else total + term
        parts[n] = total
    prod = jnp.sum(parts[...], axis=1) * active
    prod_out[...] = prod
    onehot = second_onehot(row, count_first, count_second)
    sums = exact_dot(jnp.concatenate([own, onehot], axis=0), prod)
    sum_out[...] = sums[:slots]
    sec_out[pl.ds(0, count_second), :] = sums[slots:]
    sec_out[pl.ds(count_second, own2), :] += prices[...]


def plan_kernel(sizes, everyone, ids, usable, total, cost, lower, upper, first,
                send_out, pick_out, square, shared):
    devices, slots, shard, most, keep, me_axes = sizes
    me = lax.axis_index(me_axes).astype(F32)
    base = me * float(shard)
    table = everyone[:, 0, :].astype(F32)
    row = ids[...]
    before = earlier(slots)
    asked = as_float((table >= base) & (table < base + float(shard)))
    rank = count_dot(asked, before)
    slot_number = iota((devices, slots), 1)
    lane = iota((devices, 128), 1)
    id_row = jnp.full((devices, 128), -1.0, F32)
    places = []
    for q in range(most):
        chosen = asked * as_float(rank == float(q))
        has = jnp.sum(chosen, axis=1, keepdims=True)
        place = jnp.sum(chosen * (table - base), axis=1, keepdims=True)
        number = jnp.sum(chosen * slot_number, axis=1, keepdims=True)
        places.append(jnp.where(has > 0.0, place, -1.0))
        id_row = jnp.where(lane == float(q), jnp.where(has > 0.0, number, -1.0), id_row)
    wanted = as_float(jnp.concatenate(places, axis=0) == iota((most * devices, shard), 1))
    for a, source in enumerate((cost, lower, upper, first)):
        answer = exact_dot(wanted, source[...])
        for q in range(most):
            send_out[:, q * 4 + a, :] = answer[q * devices : (q + 1) * devices]
    square[...] = jnp.full_like(square, -5.0)
    square[pl.ds(0, devices), pl.ds(0, slots)] = table
    turned = jnp.transpose(square[...])
    for e in range(devices):
        named = as_float(turned[:slots, e : e + 1] == row)
        shared[pl.ds(e, 1), :] = jnp.max(named, axis=0, keepdims=True) * usable[...]
    both = shared[...] * as_float(iota((devices, slots), 0) != me)
    count = jnp.max(jnp.sum(both, axis=1, keepdims=True), axis=0, keepdims=True)
    id_row = jnp.where(lane == float(most + keep), as_float(count > float(keep)), id_row)
    rank = count_dot(both, before)
    picks = []
    for p in range(keep):
        chosen = both * as_float(rank == float(p))
        has = jnp.sum(chosen, axis=1, keepdims=True)
        name = jnp.sum(chosen * row, axis=1, keepdims=True)
        id_row = jnp.where(lane == float(most + p), jnp.where(has > 0.0, name, -1.0), id_row)
        picks.append(chosen)
    pick = jnp.concatenate(picks, axis=0)
    pick_out[...] = pick
    rows = exact_dot(pick, total[...])
    for p in range(keep):
        send_out[:, most * 4 + p, :] = rows[p * devices : (p + 1) * devices]
    send_out[:, most * 4 + keep, :] = id_row


def side_kernel(sizes, everyone, ids, own, pick, cost, lower, upper, first, blocks_in, used,
                base_out, place_out, reply_out, stack_out, kept_out, scale_out, tops, blocks, block_sems):
    devices, slots, shard, most, me_axes = sizes
    wait = fetch_blocks(blocks_in, blocks, block_sems)
    base = lax.axis_index(me_axes).astype(F32) * float(shard)
    table = everyone[:, 0, :].astype(F32)
    row = ids[...]
    before = earlier(slots)
    asked = as_float((table >= base) & (table < base + float(shard)))
    rank = count_dot(asked, before)
    places = []
    for q in range(most):
        chosen = asked * as_float(rank == float(q))
        has = jnp.sum(chosen, axis=1, keepdims=True)
        place = jnp.sum(chosen * (table - base), axis=1, keepdims=True)
        places.append(jnp.where(has > 0.0, place, -1.0))
    wanted = as_float(jnp.concatenate(places, axis=0) == iota((most * devices, shard), 1))
    below = as_float(iota((most * devices, most * devices), 0) > iota((most * devices, most * devices), 1))
    wanted = wanted * as_float(count_dot(below, wanted) == 0.0)
    place_out[...] = wanted
    touched = exact_dot(wanted, jnp.ones((most * devices, cost.shape[1]), F32), (0, 0))
    x = first[...]
    for _ in range(ITERS):
        x = jnp.clip(x - STEP_PRIMAL * cost[...], lower[...], upper[...])
    base_out[...] = jnp.where(touched > 0.0, 0.0, x)
    owner = iota((devices, slots), 0) * float(shard)
    held = as_float((row >= owner) & (row < owner + float(shard)))
    rank = count_dot(held, before)
    for q in range(most):
        reply_out[pl.ds(q * devices, devices), :] = held * as_float(rank == float(q))
    stack_out[pl.ds(0, slots), :] = own[...]
    stack_out[pl.ds(slots, pick.shape[0]), :] = count_dot(pick[...], own[...])
    tile = blocks.shape[1]
    for n in range(slots):
        wait(n)
        top = None
        for i in range(tile // 8):
            size = jnp.abs(blocks[n, pl.ds(i * 8, 8), :])
            top = size if top is None else jnp.maximum(top, size)
        tops[n] = top
    top = jnp.max(jnp.max(tops[...], axis=1), axis=1, keepdims=True)
    factors = jnp.broadcast_to(jnp.where(top > 1e-30, 32767.0 / jnp.maximum(top, 1e-30), 0.0), (slots, tile))
    active = as_float(iota((slots, tile), 0) < used[0, 0].astype(F32))
    scale_out[...] = jnp.broadcast_to(top, (slots, tile)) * (1.0 / 32767.0) * active
    for n in range(slots):
        factor = jnp.broadcast_to(factors[n : n + 1, :], (16, tile))
        for i in range(tile // 16):
            part = pl.ds(i * 16, 16)
            level = jnp.floor(blocks[n, part, :] * factor + 0.5)
            kept_out[n, part, :] = level.astype(jnp.int32).astype(jnp.int16)


def step_kernel(sizes, first_step, last_step, direct, *refs):
    devices, slots, count_first, count_second, own2, peers, most, keep, cells = sizes
    refs = list(refs)
    take = lambda: refs.pop(0)
    kept, scale, rows, ids, dual_t, bound_t = [take() for _ in range(6)]
    row = ids[...]
    if first_step:
        answer = take()
        own_sum = None if direct else take()
        gradient = take() if direct else None
        sec_own = take()
        sec_in = [take() for _ in range(len(peers))]
    else:
        x_in, cost_in, lower_in, upper_in, match_in = take(), take(), take(), take(), take()
        y_in, cost2_in, upper2_in = take(), take(), take()
        if direct:
            gradient = take()
        else:
            own_sum, received = take(), take()
        sec_own = take()
        sec_in = [take() for _ in range(len(peers))]
    if not last_step:
        if not direct:
            stack_in = take()
    else:
        reply_in = take()
        squares_in = [take() for _ in range(ITERS - 1)]
    if first_step:
        cost_out, lower_out, upper_out, match_out, cost2_out, upper2_out = [take() for _ in range(6)]
        flag_out = None if direct else take()
    if last_step:
        reply_out, y_out, dual_out = take(), take(), take()
    else:
        x_out, y_out, dual_out, square_out, sec_out, sum_out = [take() for _ in range(6)]
        send_out = None if direct else take()
    spread, parts, second_all = take(), take(), take()
    accs = [take() for _ in range(ACCS)]
    square = take()

    if first_step:
        me2 = lax.axis_index(PAIR)
        for k, source in [(0, sec_own)] + list(zip(peers, sec_in)):
            place = pl.multiple_of(lax.bitwise_xor(me2, k) * own2, own2)
            for a in range(3):
                second_all[a, pl.ds(place, own2), :] = source[pl.ds(count_second + a * own2, own2), :]
        cost2, upper2, y = second_all[0], second_all[1], second_all[2]
        cost2_out[...] = cost2
        upper2_out[...] = upper2
        id_row = answer[:, most * 4 + keep, :]
        names = jnp.concatenate([id_row[:, q : q + 1] for q in range(most)], axis=0)
        place = as_float(names == iota((most * devices, slots), 1))
        got = []
        for a in range(4):
            stacked = jnp.concatenate([answer[:, q * 4 + a, :] for q in range(most)], axis=0)
            got.append(exact_dot(place, stacked, (0, 0)))
        cost, lower, upper, x = got
        cost_out[...] = cost
        lower_out[...] = lower
        upper_out[...] = upper
        names = jnp.concatenate([id_row[:, most + p : most + p + 1] for p in range(keep)], axis=0)
        match = as_float(names == row)
        match_out[...] = match
        if not direct:
            flag_out[0, 0] = jnp.where(jnp.max(id_row[:, most + keep : most + keep + 1]) > 0.5, 1, 0)
            fresh = jnp.concatenate([answer[:, most * 4 + p, :] for p in range(keep)], axis=0)
    else:
        x, cost, lower, upper, match = x_in[...], cost_in[...], lower_in[...], upper_in[...], match_in[...]
        y, cost2, upper2 = y_in[...], cost2_in[...], upper2_in[...]
        if not direct:
            fresh = jnp.concatenate([received[:, p, :] for p in range(keep)], axis=0)
    if direct:
        grad = gradient[...]
    else:
        grad = own_sum[...] + exact_dot(match, fresh, (0, 0))
    grad2 = sec_own[pl.ds(0, count_second), :]
    for source in sec_in:
        grad2 = grad2 + source[pl.ds(0, count_second), :]
    x_next = jnp.clip(x - STEP_PRIMAL * (cost - grad), lower, upper)
    y_next = jnp.clip(y - STEP_PRIMAL * (cost2 - grad2), 0.0, upper2)
    onehot = second_onehot(row, count_first, count_second)
    bars = ((2.0 * x_next - x) + exact_dot(onehot, 2.0 * y_next - y, (0, 0))) * scale[...]
    if last_step:
        parts_y = second_all.at[0]
        parts_y[...] = y_next
        y_out[0] = parts_y[pl.ds(pl.multiple_of(lax.axis_index(PAIR) * own2, own2), own2), :]
    else:
        y_out[...] = y_next
    for acc in accs:
        acc[...] = jnp.zeros_like(acc)
    tile = kept.shape[1]
    for n in range(slots):
        r = rows[0, n]
        acc = accs[n % ACCS]
        bar = jnp.broadcast_to(bars[n : n + 1, :], (16, tile))
        for i in range(tile // 16):
            part = pl.ds(i * 16, 16)
            acc[r, part, :] += kept[n, part, :].astype(F32) * bar
    local_rows = spread.shape[0]
    duals = dual_t[...]
    bounds = bound_t[...]
    lane = lax.broadcasted_iota(jnp.int32, (tile, tile), 1)
    next_dual = jnp.zeros((tile, tile), F32)
    squares = jnp.zeros((tile, 1), F32)
    for r in range(local_rows):
        total = accs[0][r]
        for acc in accs[1:]:
            total = total + acc[r]
        residual = bounds[:, r : r + 1] - jnp.sum(total, axis=1, keepdims=True)
        squares = squares + residual * residual
        column = jnp.maximum(duals[:, r : r + 1] + STEP_DUAL * residual, 0.0)
        wide = jnp.broadcast_to(column, (tile, tile))
        spread[r] = wide
        next_dual = jnp.where(lane == r, wide, next_dual)
    squares = jnp.broadcast_to(jnp.sum(squares, axis=0, keepdims=True), (1, tile))
    if last_step:
        square[...] = jnp.transpose(next_dual)
        dual_out[0] = square[pl.ds(0, local_rows), :]
        lanes = lax.broadcasted_iota(jnp.int32, (1, tile), 1)
        note = jnp.zeros((1, tile), F32)
        for k, value in enumerate([s[...] for s in squares_in] + [squares]):
            note = jnp.where(lanes == k, value, note)
        reply = exact_dot(reply_in[...], x_next)
        for q in range(most):
            reply_out[:, q, :] = reply[q * devices : (q + 1) * devices]
        reply_out[:, most, :] = jnp.broadcast_to(note, (devices, tile))
    else:
        x_out[...] = x_next
        dual_out[...] = next_dual
        square_out[...] = squares
        prod = adjoint_products(kept, rows, spread, parts) * scale[...]
        if direct:
            sec_out[...] = exact_dot(onehot, prod)
            sum_out[...] = prod
        else:
            out = exact_dot(jnp.concatenate([stack_in[...], onehot], axis=0), prod)
            sum_out[...] = out[:slots]
            for p in range(keep):
                send_out[:, p, :] = out[slots + p * devices : slots + (p + 1) * devices]
            sec_out[...] = out[slots + keep * devices :]


def finish_kernel(sizes, reply, base, place, first_out, norm_out):
    devices, most, cells = sizes
    rows = jnp.concatenate([reply[:, q, :] for q in range(most)], axis=0)
    first_out[...] = base[...] + exact_dot(place[...], rows, (0, 0))
    norms = jnp.sqrt(jnp.sum(reply[:, most, :], axis=0, keepdims=True) / float(cells))
    lane = lax.broadcasted_iota(jnp.int32, norms.shape, 1)
    for k in range(ITERS):
        norm_out[k] = jnp.max(jnp.where(lane == k, norms, 0.0))


def shards(
    block_matrices,
    slot_row_block,
    tile_column,
    block_count,
    carbon_scenario,
    intensity,
    cost_first,
    lower_first,
    upper_first,
    cost_second,
    upper_second,
    row_bound,
    first_start,
    second_start,
    dual_start,
):
    devices = lax.axis_size(GROUP)
    pairs = lax.axis_size(PAIR)
    scenarios, slots = slot_row_block.shape
    local_rows, tile = row_bound.shape[1:]
    shard = cost_first.shape[0]
    own2 = cost_second.shape[1]
    count_first = shard * devices
    count_second = own2 * pairs
    cells = scenarios * local_rows * tile * devices
    most = -(-scenarios * slots // devices)
    keep = SHARED
    peers = list(range(1, pairs))

    def shape(*dims):
        return jax.ShapeDtypeStruct(dims, F32)

    def scratch(*dims):
        return pltpu.VMEM(dims, F32)

    params = pltpu.CompilerParams(vmem_limit_bytes=16 << 20)

    def call(kernel, outs, specs, name, *args, scratches=(), out_specs=None):
        return pl.pallas_call(
            kernel,
            out_shape=tuple(outs),
            in_specs=specs,
            out_specs=tuple(out_specs or [VM] * len(outs)),
            scratch_shapes=list(scratches),
            compiler_params=params,
            name=name,
        )(*args)

    def far(value):
        return pltpu.with_memory_space_constraint(value, pltpu.HBM)

    def near(value):
        return pltpu.with_memory_space_constraint(value, pltpu.VMEM)

    block_scratch = [scratch(slots, tile, tile), pltpu.SemaphoreType.DMA((slots // CHUNK,))]
    blocks = far(block_matrices[0])
    everyone = lax.all_to_all(
        jnp.broadcast_to(tile_column[None], (devices, 1, slots)), GROUP, 0, 0, tiled=True
    )
    ids, prod, sec, dual_t, bound_t, own, own_sum, usable = call(
        functools.partial(start_kernel, (tile, own2, count_first, count_second)),
        [shape(1, slots), shape(slots, tile), shape(count_second + 3 * own2, tile), shape(tile, tile),
         shape(tile, tile), shape(slots, slots), shape(slots, tile), shape(1, slots)],
        [HB, SM, SM, VM] + [HB] * 6 + [SM],
        "start",
        blocks, slot_row_block, block_count, tile_column, far(dual_start[0]), far(row_bound[0]), far(cost_second[0]),
        far(upper_second[0]), far(second_start[0]), far(intensity), carbon_scenario,
        scratches=[scratch(local_rows, tile, tile), scratch(slots, 8, tile), scratch(2, tile, tile),
                   scratch(own2, tile), block_scratch[0], pltpu.SemaphoreType.DMA((6,)), block_scratch[1]],
    )
    firsts = (cost_first, lower_first, upper_first, first_start)
    width = -(-(most * 4 + keep + 1) // 8) * 8
    send, pick = call(
        functools.partial(plan_kernel, (devices, slots, shard, most, keep, GROUP)),
        [shape(devices, width, tile), shape(keep * devices, slots)],
        [VM] * 8,
        "plan",
        everyone, ids, usable, own_sum, *firsts,
        scratches=[scratch(128, 128), scratch(devices, slots)],
    )
    answer = lax.all_to_all(send, GROUP, 0, 0, tiled=True)
    base, place, reply_pick, stack, kept, scale = call(
        functools.partial(side_kernel, (devices, slots, shard, most, GROUP)),
        [shape(shard, tile), shape(most * devices, shard), shape(most * devices, slots),
         shape(slots + keep * devices, slots), pltpu.VMEM((slots, tile, tile), jnp.int16), shape(slots, tile)],
        [VM] * 8 + [HB, SM],
        "side",
        everyone, ids, own, pick, *firsts, blocks, block_count,
        scratches=[scratch(slots, 8, tile)] + block_scratch,
    )

    def swap(value):
        return [lax.ppermute(value, PAIR, [(i, i ^ k) for i in range(pairs)]) for k in peers]

    sec_in = swap(sec)
    step_sizes = (devices, slots, count_first, count_second, own2, peers, most, keep, cells)
    step_scratch = (
        [scratch(local_rows, tile, tile), scratch(slots, 8, tile), scratch(3, count_second, tile)]
        + [scratch(local_rows, tile, tile)] * ACCS
        + [scratch(tile, tile)]
    )
    reply_width = -(-(most + 1) // 8) * 8

    def exchange(value):
        gathered = lax.all_gather(value, GROUP, axis=0, tiled=True)
        match = (everyone.astype(F32).reshape(1, -1) == ids.reshape(-1, 1)).astype(F32)
        return jnp.dot(match, gathered, precision=lax.Precision.HIGHEST)

    def run_step(step, direct, args):
        first_step, last_step = step == 0, step == ITERS - 1
        if last_step:
            outs = [shape(devices, reply_width, tile), shape(1, own2, tile), shape(1, local_rows, tile)]
        else:
            outs = [shape(slots, tile), shape(count_second, tile), shape(tile, tile), shape(1, tile),
                    shape(count_second, tile), shape(slots, tile)]
            if not direct:
                outs.append(shape(devices, keep, tile))
        specs = [VM] * len(outs)
        if first_step:
            lead = [shape(slots, tile)] * 3 + [shape(keep * devices, slots)] + [shape(count_second, tile)] * 2
            lead_specs = [VM] * 6
            if not direct:
                lead.append(jax.ShapeDtypeStruct((1, 1), jnp.int32))
                lead_specs.append(SM)
            outs, specs = lead + outs, lead_specs + specs
        return list(call(
            functools.partial(step_kernel, step_sizes, first_step, last_step, direct),
            outs,
            [VM, VM, SM] + [VM] * (len(args) - 3),
            "step",
            *args,
            scratches=step_scratch,
            out_specs=specs,
        ))

    def begin(direct, answer, own_sum, dual_t, sec, sec_in):
        args = [near(kept), scale, slot_row_block, ids, dual_t, bound_t, answer, own_sum, sec] + list(sec_in)
        if not direct:
            args.append(stack)
        return run_step(0, direct, args)

    def proceed(direct, fixed, state):
        squares = []
        for step in range(1, ITERS):
            x, y, dual_t, square, sec, own_sum = state[:6]
            squares.append(square)
            cost, lower, upper, match, cost2, upper2 = fixed
            args = [near(kept), scale, slot_row_block, ids, dual_t, bound_t, x, cost, lower, upper, match, y, cost2, upper2]
            if direct:
                args.append(exchange(own_sum))
            else:
                args += [own_sum, lax.all_to_all(state[6], GROUP, 0, 0, tiled=True)]
            args += [sec] + swap(sec)
            if step == ITERS - 1:
                args += [reply_pick] + squares
            elif not direct:
                args.append(stack)
            state = run_step(step, direct, args)
        reply, y, dual = state
        return lax.all_to_all(reply, GROUP, 0, 0, tiled=True), y, dual

    def general(operands):
        (answer, prod, dual_t, sec, sec_in), _ = operands
        results = begin(True, answer, exchange(prod), dual_t, sec, sec_in)
        return proceed(True, results[:6], results[6:])

    def usual(operands):
        _, results = operands
        return proceed(False, results[:6], results[7:])

    results = begin(False, answer, own_sum, dual_t, sec, sec_in)
    reply, y, dual = lax.cond(
        results[6][0, 0] > 0, general, usual, ((answer, prod, dual_t, sec, sec_in), results)
    )
    first_final, norms = call(
        functools.partial(finish_kernel, (devices, most, cells)),
        [shape(shard, tile), shape(ITERS)],
        [VM] * 3,
        "finish",
        reply, base, place,
        out_specs=[VM, SM],
    )
    return first_final, y, dual, norms


def solution(mesh):
    return jax.shard_map(
        shards,
        mesh=mesh,
        in_specs=(
            P(("grp", "scen"), ("blk", "sub"), None, None),
            P(("grp", "scen"), ("blk", "sub")),
            P(("grp", "scen"), ("blk", "sub")),
            P(("grp", "scen"), ("blk", "sub")),
            P(("grp", "scen")),
            P(None, ("blk", "sub"), None),
            P(("grp", "scen", "blk", "sub"), None),
            P(("grp", "scen", "blk", "sub"), None),
            P(("grp", "scen", "blk", "sub"), None),
            P(("grp", "scen"), ("blk", "sub"), None),
            P(("grp", "scen"), ("blk", "sub"), None),
            P(("grp", "scen"), ("blk", "sub"), None),
            P(("grp", "scen", "blk", "sub"), None),
            P(("grp", "scen"), ("blk", "sub"), None),
            P(("grp", "scen"), ("blk", "sub"), None),
        ),
        out_specs=(
            P(("grp", "scen", "blk", "sub"), None),
            P(("grp", "scen"), ("blk", "sub"), None),
            P(("grp", "scen"), ("blk", "sub"), None),
            P("grp"),
        ),
        check_vma=False,
    )
```

```python
import functools

import jax
import jax.numpy as jnp
from jax import lax
from jax.experimental import pallas as pl
from jax.experimental.pallas import tpu as pltpu
from jax.sharding import PartitionSpec as P

ITERS = 3
STEP_PRIMAL = 0.4
STEP_DUAL = 0.4
SHARED = 4
GROUP = ("scen", "blk", "sub")
PAIR = ("blk", "sub")
F32 = jnp.float32
VM = pl.BlockSpec(memory_space=pltpu.VMEM)
SM = pl.BlockSpec(memory_space=pltpu.SMEM)
HB = pl.BlockSpec(memory_space=pl.ANY)
ACCS = 2
CHUNK = 16


def exact_dot(a, b, contract=(1, 0)):
    dims = (((contract[0],), (contract[1],)), ((), ()))
    high = b.astype(jnp.bfloat16)
    rest = b - high.astype(F32)
    middle = rest.astype(jnp.bfloat16)
    low = (rest - middle.astype(F32)).astype(jnp.bfloat16)
    parts = jnp.concatenate([high, middle, low], axis=1)
    out = lax.dot_general(a.astype(jnp.bfloat16), parts, dims, preferred_element_type=F32)
    width = b.shape[1]
    return out[:, :width] + (out[:, width : 2 * width] + out[:, 2 * width :])


def count_dot(a, b):
    return jnp.dot(a.astype(jnp.bfloat16), b.astype(jnp.bfloat16), preferred_element_type=F32)


def iota(shape, dim):
    return lax.broadcasted_iota(jnp.int32, shape, dim).astype(F32)


def as_float(flags):
    return jnp.where(flags, 1.0, 0.0).astype(F32)


def earlier(size):
    return as_float(iota((size, size), 0) < iota((size, size), 1))


def second_onehot(ids_row, count_first, count_second):
    slots = ids_row.shape[1]
    return as_float(ids_row - float(count_first) == iota((count_second, slots), 0))


def fetch_blocks(source, target, sems):
    copies = [
        pltpu.make_async_copy(source.at[pl.ds(k, CHUNK)], target.at[pl.ds(k, CHUNK)], sems.at[k // CHUNK])
        for k in range(0, target.shape[0], CHUNK)
    ]
    for copy in copies:
        copy.start()

    def wait(n):
        if n % CHUNK == 0:
            copies[n // CHUNK].wait()

    return wait


def adjoint_products(kept, rows, spread, parts):
    slots, tile, _ = kept.shape
    for n in range(slots):
        row = rows[0, n]
        total = None
        for i in range(tile // 16):
            part = pl.ds(i * 16, 16)
            term = kept[n, part, :].astype(F32) * spread[row, part, :]
            total = term if total is None else total + term
        parts[n] = total[:8] + total[8:]
    return jnp.sum(parts[...], axis=1)


def spread_duals(dual_t, spread):
    tile = spread.shape[1]
    for r in range(spread.shape[0]):
        spread[r] = jnp.broadcast_to(dual_t[:, r : r + 1], (tile, tile))


def start_kernel(sizes, blocks_in, rows_in, used, columns, dual, bound, cost2, upper2, second, intensity, carbon,
                 ids_out, prod_out, sec_out, dual_out, bound_out, own_out, sum_out, usable_out,
                 spread, parts, squares, prices, rows, blocks, sems, block_sems):
    tile, own2, count_first, count_second = sizes
    slots = blocks.shape[0]
    local_rows = dual.shape[0]
    places = [sec_out.at[pl.ds(count_second + a * own2, own2), :] for a in range(3)]
    copies = [
        pltpu.make_async_copy(source, target, sems.at[k])
        for k, (source, target) in enumerate([
            (dual, squares.at[0, pl.ds(0, local_rows), :]),
            (bound, squares.at[1, pl.ds(0, local_rows), :]),
            (cost2, places[0]),
            (upper2, places[1]),
            (second, places[2]),
            (intensity.at[carbon[0]], prices),
            (rows_in, rows),
        ])
    ]
    for copy in copies:
        copy.start()
    wait = fetch_blocks(blocks_in, blocks, block_sems)
    row = columns[...].astype(F32)
    ids_out[...] = row
    active = as_float(iota((slots, tile), 0) < used[0, 0].astype(F32))
    eye = as_float(iota((slots, slots), 0) == iota((slots, slots), 1))
    column = jnp.sum(eye * row, axis=1, keepdims=True)
    own = as_float(column == row)
    own_out[...] = own
    again = jnp.max(own * earlier(slots), axis=0, keepdims=True)
    some = jnp.max(own * active[:, :1], axis=0, keepdims=True)
    usable_out[...] = as_float(row < float(count_first)) * (1.0 - again) * some
    for k in range(2):
        squares[k, pl.ds(local_rows, tile - local_rows), :] = jnp.zeros((tile - local_rows, tile), F32)
    for copy in copies:
        copy.wait()
    for k, target in enumerate((dual_out, bound_out)):
        target[...] = jnp.transpose(squares[k])
    spread_duals(dual_out[...], spread)
    for n in range(slots):
        wait(n)
        r = rows[0, n]
        total = None
        for i in range(tile // 8):
            term = blocks[n, pl.ds(i * 8, 8), :] * spread[r, pl.ds(i * 8, 8), :]
            total = term if total is None else total + term
        parts[n] = total
    prod = jnp.sum(parts[...], axis=1) * active
    prod_out[...] = prod
    onehot = second_onehot(row, count_first, count_second)
    sums = exact_dot(jnp.concatenate([own, onehot], axis=0), prod)
    sum_out[...] = sums[:slots]
    sec_out[pl.ds(0, count_second), :] = sums[slots:]
    sec_out[pl.ds(count_second, own2), :] += prices[...]


def plan_kernel(sizes, everyone, ids, usable, total, cost, lower, upper, first,
                send_out, pick_out, square, shared):
    devices, slots, shard, most, keep, me_axes = sizes
    me = lax.axis_index(me_axes).astype(F32)
    base = me * float(shard)
    table = everyone[:, 0, :].astype(F32)
    row = ids[...]
    before = earlier(slots)
    asked = as_float((table >= base) & (table < base + float(shard)))
    rank = count_dot(asked, before)
    slot_number = iota((devices, slots), 1)
    lane = iota((devices, 128), 1)
    id_row = jnp.full((devices, 128), -1.0, F32)
    places = []
    for q in range(most):
        chosen = asked * as_float(rank == float(q))
        has = jnp.sum(chosen, axis=1, keepdims=True)
        place = jnp.sum(chosen * (table - base), axis=1, keepdims=True)
        number = jnp.sum(chosen * slot_number, axis=1, keepdims=True)
        places.append(jnp.where(has > 0.0, place, -1.0))
        id_row = jnp.where(lane == float(q), jnp.where(has > 0.0, number, -1.0), id_row)
    wanted = as_float(jnp.concatenate(places, axis=0) == iota((most * devices, shard), 1))
    for a, source in enumerate((cost, lower, upper, first)):
        answer = exact_dot(wanted, source[...])
        for q in range(most):
            send_out[:, q * 4 + a, :] = answer[q * devices : (q + 1) * devices]
    square[...] = jnp.full_like(square, -5.0)
    square[pl.ds(0, devices), pl.ds(0, slots)] = table
    turned = jnp.transpose(square[...])
    for e in range(devices):
        named = as_float(turned[:slots, e : e + 1] == row)
        shared[pl.ds(e, 1), :] = jnp.max(named, axis=0, keepdims=True) * usable[...]
    both = shared[...] * as_float(iota((devices, slots), 0) != me)
    count = jnp.max(jnp.sum(both, axis=1, keepdims=True), axis=0, keepdims=True)
    id_row = jnp.where(lane == float(most + keep), as_float(count > float(keep)), id_row)
    rank = count_dot(both, before)
    picks = []
    for p in range(keep):
        chosen = both * as_float(rank == float(p))
        has = jnp.sum(chosen, axis=1, keepdims=True)
        name = jnp.sum(chosen * row, axis=1, keepdims=True)
        id_row = jnp.where(lane == float(most + p), jnp.where(has > 0.0, name, -1.0), id_row)
        picks.append(chosen)
    pick = jnp.concatenate(picks, axis=0)
    pick_out[...] = pick
    rows = exact_dot(pick, total[...])
    for p in range(keep):
        send_out[:, most * 4 + p, :] = rows[p * devices : (p + 1) * devices]
    send_out[:, most * 4 + keep, :] = id_row


def side_kernel(sizes, everyone, ids, own, pick, cost, lower, upper, first, blocks_in, used,
                base_out, place_out, reply_out, stack_out, kept_out, scale_out, tops, blocks, block_sems):
    devices, slots, shard, most, me_axes = sizes
    wait = fetch_blocks(blocks_in, blocks, block_sems)
    base = lax.axis_index(me_axes).astype(F32) * float(shard)
    table = everyone[:, 0, :].astype(F32)
    row = ids[...]
    before = earlier(slots)
    asked = as_float((table >= base) & (table < base + float(shard)))
    rank = count_dot(asked, before)
    places = []
    for q in range(most):
        chosen = asked * as_float(rank == float(q))
        has = jnp.sum(chosen, axis=1, keepdims=True)
        place = jnp.sum(chosen * (table - base), axis=1, keepdims=True)
        places.append(jnp.where(has > 0.0, place, -1.0))
    wanted = as_float(jnp.concatenate(places, axis=0) == iota((most * devices, shard), 1))
    below = as_float(iota((most * devices, most * devices), 0) > iota((most * devices, most * devices), 1))
    wanted = wanted * as_float(count_dot(below, wanted) == 0.0)
    place_out[...] = wanted
    touched = exact_dot(wanted, jnp.ones((most * devices, cost.shape[1]), F32), (0, 0))
    x = first[...]
    for _ in range(ITERS):
        x = jnp.clip(x - STEP_PRIMAL * cost[...], lower[...], upper[...])
    base_out[...] = jnp.where(touched > 0.0, 0.0, x)
    owner = iota((devices, slots), 0) * float(shard)
    held = as_float((row >= owner) & (row < owner + float(shard)))
    rank = count_dot(held, before)
    for q in range(most):
        reply_out[pl.ds(q * devices, devices), :] = held * as_float(rank == float(q))
    stack_out[pl.ds(0, slots), :] = own[...]
    stack_out[pl.ds(slots, pick.shape[0]), :] = count_dot(pick[...], own[...])
    tile = blocks.shape[1]
    for n in range(slots):
        wait(n)
        top = None
        for i in range(tile // 8):
            size = jnp.abs(blocks[n, pl.ds(i * 8, 8), :])
            top = size if top is None else jnp.maximum(top, size)
        tops[n] = top
    top = jnp.max(jnp.max(tops[...], axis=1), axis=1, keepdims=True)
    factors = jnp.broadcast_to(jnp.where(top > 1e-30, 32767.0 / jnp.maximum(top, 1e-30), 0.0), (slots, tile))
    active = as_float(iota((slots, tile), 0) < used[0, 0].astype(F32))
    scale_out[...] = jnp.broadcast_to(top, (slots, tile)) * (1.0 / 32767.0) * active
    for n in range(slots):
        factor = jnp.broadcast_to(factors[n : n + 1, :], (16, tile))
        for i in range(tile // 16):
            part = pl.ds(i * 16, 16)
            level = jnp.floor(blocks[n, part, :] * factor + 0.5)
            kept_out[n, part, :] = level.astype(jnp.int32).astype(jnp.int16)


def step_kernel(sizes, first_step, last_step, direct, *refs):
    devices, slots, count_first, count_second, own2, peers, most, keep, cells = sizes
    refs = list(refs)
    take = lambda: refs.pop(0)
    kept, scale, rows_in, ids, dual_t, bound_t = [take() for _ in range(6)]
    row = ids[...]
    if first_step:
        answer = take()
        own_sum = None if direct else take()
        gradient = take() if direct else None
        sec_own = take()
        sec_in = [take() for _ in range(len(peers))]
    else:
        x_in, cost_in, lower_in, upper_in, match_in = take(), take(), take(), take(), take()
        y_in, cost2_in, upper2_in = take(), take(), take()
        if direct:
            gradient = take()
        else:
            own_sum, received = take(), take()
        sec_own = take()
        sec_in = [take() for _ in range(len(peers))]
    if not last_step:
        if not direct:
            stack_in = take()
    else:
        reply_in = take()
        squares_in = [take() for _ in range(ITERS - 1)]
    if first_step:
        cost_out, lower_out, upper_out, match_out, cost2_out, upper2_out = [take() for _ in range(6)]
        flag_out = None if direct else take()
    if last_step:
        reply_out, y_out, dual_out = take(), take(), take()
    else:
        x_out, y_out, dual_out, square_out, sec_out, sum_out = [take() for _ in range(6)]
        send_out = None if direct else take()
    spread, parts, second_all = take(), take(), take()
    accs = [take() for _ in range(ACCS)]
    square, rows, row_sems = take(), take(), take()
    row_copy = pltpu.make_async_copy(rows_in, rows, row_sems.at[0])
    row_copy.start()

    if first_step:
        me2 = lax.axis_index(PAIR)
        for k, source in [(0, sec_own)] + list(zip(peers, sec_in)):
            place = pl.multiple_of(lax.bitwise_xor(me2, k) * own2, own2)
            for a in range(3):
                second_all[a, pl.ds(place, own2), :] = source[pl.ds(count_second + a * own2, own2), :]
        cost2, upper2, y = second_all[0], second_all[1], second_all[2]
        cost2_out[...] = cost2
        upper2_out[...] = upper2
        id_row = answer[:, most * 4 + keep, :]
        names = jnp.concatenate([id_row[:, q : q + 1] for q in range(most)], axis=0)
        place = as_float(names == iota((most * devices, slots), 1))
        got = []
        for a in range(4):
            stacked = jnp.concatenate([answer[:, q * 4 + a, :] for q in range(most)], axis=0)
            got.append(exact_dot(place, stacked, (0, 0)))
        cost, lower, upper, x = got
        cost_out[...] = cost
        lower_out[...] = lower
        upper_out[...] = upper
        names = jnp.concatenate([id_row[:, most + p : most + p + 1] for p in range(keep)], axis=0)
        match = as_float(names == row)
        match_out[...] = match
        if not direct:
            flag_out[0, 0] = jnp.where(jnp.max(id_row[:, most + keep : most + keep + 1]) > 0.5, 1, 0)
            fresh = jnp.concatenate([answer[:, most * 4 + p, :] for p in range(keep)], axis=0)
    else:
        x, cost, lower, upper, match = x_in[...], cost_in[...], lower_in[...], upper_in[...], match_in[...]
        y, cost2, upper2 = y_in[...], cost2_in[...], upper2_in[...]
        if not direct:
            fresh = jnp.concatenate([received[:, p, :] for p in range(keep)], axis=0)
    if direct:
        grad = gradient[...]
    else:
        grad = own_sum[...] + exact_dot(match, fresh, (0, 0))
    grad2 = sec_own[pl.ds(0, count_second), :]
    for source in sec_in:
        grad2 = grad2 + source[pl.ds(0, count_second), :]
    x_next = jnp.clip(x - STEP_PRIMAL * (cost - grad), lower, upper)
    y_next = jnp.clip(y - STEP_PRIMAL * (cost2 - grad2), 0.0, upper2)
    onehot = second_onehot(row, count_first, count_second)
    bars = ((2.0 * x_next - x) + exact_dot(onehot, 2.0 * y_next - y, (0, 0))) * scale[...]
    if last_step:
        parts_y = second_all.at[0]
        parts_y[...] = y_next
        y_out[0] = parts_y[pl.ds(pl.multiple_of(lax.axis_index(PAIR) * own2, own2), own2), :]
    else:
        y_out[...] = y_next
    for acc in accs:
        acc[...] = jnp.zeros_like(acc)
    tile = kept.shape[1]
    row_copy.wait()
    for n in range(slots):
        r = rows[0, n]
        acc = accs[n % ACCS]
        bar = jnp.broadcast_to(bars[n : n + 1, :], (16, tile))
        for i in range(tile // 16):
            part = pl.ds(i * 16, 16)
            acc[r, part, :] += kept[n, part, :].astype(F32) * bar
    local_rows = spread.shape[0]
    duals = dual_t[...]
    bounds = bound_t[...]
    lane = lax.broadcasted_iota(jnp.int32, (tile, tile), 1)
    next_dual = jnp.zeros((tile, tile), F32)
    squares = jnp.zeros((tile, 1), F32)
    for r in range(local_rows):
        total = accs[0][r]
        for acc in accs[1:]:
            total = total + acc[r]
        residual = bounds[:, r : r + 1] - jnp.sum(total, axis=1, keepdims=True)
        squares = squares + residual * residual
        column = jnp.maximum(duals[:, r : r + 1] + STEP_DUAL * residual, 0.0)
        wide = jnp.broadcast_to(column, (tile, tile))
        spread[r] = wide
        next_dual = jnp.where(lane == r, wide, next_dual)
    squares = jnp.broadcast_to(jnp.sum(squares, axis=0, keepdims=True), (1, tile))
    if last_step:
        square[...] = jnp.transpose(next_dual)
        dual_out[0] = square[pl.ds(0, local_rows), :]
        lanes = lax.broadcasted_iota(jnp.int32, (1, tile), 1)
        note = jnp.zeros((1, tile), F32)
        for k, value in enumerate([s[...] for s in squares_in] + [squares]):
            note = jnp.where(lanes == k, value, note)
        reply = exact_dot(reply_in[...], x_next)
        for q in range(most):
            reply_out[:, q, :] = reply[q * devices : (q + 1) * devices]
        reply_out[:, most, :] = jnp.broadcast_to(note, (devices, tile))
    else:
        x_out[...] = x_next
        dual_out[...] = next_dual
        square_out[...] = squares
        prod = adjoint_products(kept, rows, spread, parts) * scale[...]
        if direct:
            sec_out[...] = exact_dot(onehot, prod)
            sum_out[...] = prod
        else:
            out = exact_dot(jnp.concatenate([stack_in[...], onehot], axis=0), prod)
            sum_out[...] = out[:slots]
            for p in range(keep):
                send_out[:, p, :] = out[slots + p * devices : slots + (p + 1) * devices]
            sec_out[...] = out[slots + keep * devices :]


def finish_kernel(sizes, reply, base, place, first_out, norm_out):
    devices, most, cells = sizes
    rows = jnp.concatenate([reply[:, q, :] for q in range(most)], axis=0)
    first_out[...] = base[...] + exact_dot(place[...], rows, (0, 0))
    norms = jnp.sqrt(jnp.sum(reply[:, most, :], axis=0, keepdims=True) / float(cells))
    lane = lax.broadcasted_iota(jnp.int32, norms.shape, 1)
    for k in range(ITERS):
        norm_out[k] = jnp.max(jnp.where(lane == k, norms, 0.0))


def shards(
    block_matrices,
    slot_row_block,
    tile_column,
    block_count,
    carbon_scenario,
    intensity,
    cost_first,
    lower_first,
    upper_first,
    cost_second,
    upper_second,
    row_bound,
    first_start,
    second_start,
    dual_start,
):
    devices = lax.axis_size(GROUP)
    pairs = lax.axis_size(PAIR)
    scenarios, slots = slot_row_block.shape
    local_rows, tile = row_bound.shape[1:]
    shard = cost_first.shape[0]
    own2 = cost_second.shape[1]
    count_first = shard * devices
    count_second = own2 * pairs
    cells = scenarios * local_rows * tile * devices
    most = -(-scenarios * slots // devices)
    keep = SHARED
    peers = list(range(1, pairs))

    def shape(*dims):
        return jax.ShapeDtypeStruct(dims, F32)

    def scratch(*dims):
        return pltpu.VMEM(dims, F32)

    params = pltpu.CompilerParams(vmem_limit_bytes=16 << 20)

    def call(kernel, outs, specs, name, *args, scratches=(), out_specs=None):
        return pl.pallas_call(
            kernel,
            out_shape=tuple(outs),
            in_specs=specs,
            out_specs=tuple(out_specs or [VM] * len(outs)),
            scratch_shapes=list(scratches),
            compiler_params=params,
            name=name,
        )(*args)

    def far(value):
        return pltpu.with_memory_space_constraint(value, pltpu.HBM)

    def near(value):
        return pltpu.with_memory_space_constraint(value, pltpu.VMEM)

    block_scratch = [scratch(slots, tile, tile), pltpu.SemaphoreType.DMA((slots // CHUNK,))]
    blocks = far(block_matrices[0])
    everyone = lax.all_to_all(
        jnp.broadcast_to(tile_column[None], (devices, 1, slots)), GROUP, 0, 0, tiled=True
    )
    ids, prod, sec, dual_t, bound_t, own, own_sum, usable = call(
        functools.partial(start_kernel, (tile, own2, count_first, count_second)),
        [shape(1, slots), shape(slots, tile), shape(count_second + 3 * own2, tile), shape(tile, tile),
         shape(tile, tile), shape(slots, slots), shape(slots, tile), shape(1, slots)],
        [HB, HB, SM, VM] + [HB] * 6 + [SM],
        "start",
        blocks, slot_row_block, block_count, tile_column, far(dual_start[0]), far(row_bound[0]), far(cost_second[0]),
        far(upper_second[0]), far(second_start[0]), far(intensity), carbon_scenario,
        scratches=[scratch(local_rows, tile, tile), scratch(slots, 8, tile), scratch(2, tile, tile),
                   scratch(own2, tile), pltpu.SMEM((1, slots), jnp.int32), block_scratch[0], pltpu.SemaphoreType.DMA((7,)), block_scratch[1]],
    )
    firsts = (cost_first, lower_first, upper_first, first_start)
    width = -(-(most * 4 + keep + 1) // 8) * 8
    send, pick = call(
        functools.partial(plan_kernel, (devices, slots, shard, most, keep, GROUP)),
        [shape(devices, width, tile), shape(keep * devices, slots)],
        [VM] * 8,
        "plan",
        everyone, ids, usable, own_sum, *firsts,
        scratches=[scratch(128, 128), scratch(devices, slots)],
    )
    answer = lax.all_to_all(send, GROUP, 0, 0, tiled=True)
    base, place, reply_pick, stack, kept, scale = call(
        functools.partial(side_kernel, (devices, slots, shard, most, GROUP)),
        [shape(shard, tile), shape(most * devices, shard), shape(most * devices, slots),
         shape(slots + keep * devices, slots), pltpu.VMEM((slots, tile, tile), jnp.int16), shape(slots, tile)],
        [VM] * 8 + [HB, SM],
        "side",
        everyone, ids, own, pick, *firsts, blocks, block_count,
        scratches=[scratch(slots, 8, tile)] + block_scratch,
    )

    def swap(value):
        return [lax.ppermute(value, PAIR, [(i, i ^ k) for i in range(pairs)]) for k in peers]

    sec_in = swap(sec)
    step_sizes = (devices, slots, count_first, count_second, own2, peers, most, keep, cells)
    step_scratch = (
        [scratch(local_rows, tile, tile), scratch(slots, 8, tile), scratch(3, count_second, tile)]
        + [scratch(local_rows, tile, tile)] * ACCS
        + [scratch(tile, tile), pltpu.SMEM((1, slots), jnp.int32), pltpu.SemaphoreType.DMA((1,))]
    )
    reply_width = -(-(most + 1) // 8) * 8

    def exchange(value):
        gathered = lax.all_gather(value, GROUP, axis=0, tiled=True)
        match = (everyone.astype(F32).reshape(1, -1) == ids.reshape(-1, 1)).astype(F32)
        return jnp.dot(match, gathered, precision=lax.Precision.HIGHEST)

    def run_step(step, direct, args):
        first_step, last_step = step == 0, step == ITERS - 1
        if last_step:
            outs = [shape(devices, reply_width, tile), shape(1, own2, tile), shape(1, local_rows, tile)]
        else:
            outs = [shape(slots, tile), shape(count_second, tile), shape(tile, tile), shape(1, tile),
                    shape(count_second, tile), shape(slots, tile)]
            if not direct:
                outs.append(shape(devices, keep, tile))
        specs = [VM] * len(outs)
        if first_step:
            lead = [shape(slots, tile)] * 3 + [shape(keep * devices, slots)] + [shape(count_second, tile)] * 2
            lead_specs = [VM] * 6
            if not direct:
                lead.append(jax.ShapeDtypeStruct((1, 1), jnp.int32))
                lead_specs.append(SM)
            outs, specs = lead + outs, lead_specs + specs
        return list(call(
            functools.partial(step_kernel, step_sizes, first_step, last_step, direct),
            outs,
            [VM, VM, HB] + [VM] * (len(args) - 3),
            "step",
            *args,
            scratches=step_scratch,
            out_specs=specs,
        ))

    def begin(direct, answer, own_sum, dual_t, sec, sec_in):
        args = [near(kept), scale, slot_row_block, ids, dual_t, bound_t, answer, own_sum, sec] + list(sec_in)
        if not direct:
            args.append(stack)
        return run_step(0, direct, args)

    def proceed(direct, fixed, state):
        squares = []
        for step in range(1, ITERS):
            x, y, dual_t, square, sec, own_sum = state[:6]
            squares.append(square)
            cost, lower, upper, match, cost2, upper2 = fixed
            args = [near(kept), scale, slot_row_block, ids, dual_t, bound_t, x, cost, lower, upper, match, y, cost2, upper2]
            if direct:
                args.append(exchange(own_sum))
            else:
                args += [own_sum, lax.all_to_all(state[6], GROUP, 0, 0, tiled=True)]
            args += [sec] + swap(sec)
            if step == ITERS - 1:
                args += [reply_pick] + squares
            elif not direct:
                args.append(stack)
            state = run_step(step, direct, args)
        reply, y, dual = state
        return lax.all_to_all(reply, GROUP, 0, 0, tiled=True), y, dual

    def general(operands):
        (answer, prod, dual_t, sec, sec_in), _ = operands
        results = begin(True, answer, exchange(prod), dual_t, sec, sec_in)
        return proceed(True, results[:6], results[6:])

    def usual(operands):
        _, results = operands
        return proceed(False, results[:6], results[7:])

    results = begin(False, answer, own_sum, dual_t, sec, sec_in)
    reply, y, dual = lax.cond(
        results[6][0, 0] > 0, general, usual, ((answer, prod, dual_t, sec, sec_in), results)
    )
    first_final, norms = call(
        functools.partial(finish_kernel, (devices, most, cells)),
        [shape(shard, tile), shape(ITERS)],
        [VM] * 3,
        "finish",
        reply, base, place,
        out_specs=[VM, SM],
    )
    return first_final, y, dual, norms


def solution(mesh):
    return jax.shard_map(
        shards,
        mesh=mesh,
        in_specs=(
            P(("grp", "scen"), ("blk", "sub"), None, None),
            P(("grp", "scen"), ("blk", "sub")),
            P(("grp", "scen"), ("blk", "sub")),
            P(("grp", "scen"), ("blk", "sub")),
            P(("grp", "scen")),
            P(None, ("blk", "sub"), None),
            P(("grp", "scen", "blk", "sub"), None),
            P(("grp", "scen", "blk", "sub"), None),
            P(("grp", "scen", "blk", "sub"), None),
            P(("grp", "scen"), ("blk", "sub"), None),
            P(("grp", "scen"), ("blk", "sub"), None),
            P(("grp", "scen"), ("blk", "sub"), None),
            P(("grp", "scen", "blk", "sub"), None),
            P(("grp", "scen"), ("blk", "sub"), None),
            P(("grp", "scen"), ("blk", "sub"), None),
        ),
        out_specs=(
            P(("grp", "scen", "blk", "sub"), None),
            P(("grp", "scen"), ("blk", "sub"), None),
            P(("grp", "scen"), ("blk", "sub"), None),
            P("grp"),
        ),
        check_vma=False,
    )
```

```python
import functools

import jax
import jax.numpy as jnp
from jax import lax
from jax.experimental import pallas as pl
from jax.experimental.pallas import tpu as pltpu
from jax.sharding import PartitionSpec as P

ITERS = 3
STEP_PRIMAL = 0.4
STEP_DUAL = 0.4
SHARED = 4
GROUP = ("scen", "blk", "sub")
PAIR = ("blk", "sub")
F32 = jnp.float32
VM = pl.BlockSpec(memory_space=pltpu.VMEM)
SM = pl.BlockSpec(memory_space=pltpu.SMEM)
HB = pl.BlockSpec(memory_space=pl.ANY)
ACCS = 1
CHUNK = 16


def exact_dot(a, b, contract=(1, 0)):
    dims = (((contract[0],), (contract[1],)), ((), ()))
    high = b.astype(jnp.bfloat16)
    rest = b - high.astype(F32)
    middle = rest.astype(jnp.bfloat16)
    low = (rest - middle.astype(F32)).astype(jnp.bfloat16)
    parts = jnp.concatenate([high, middle, low], axis=1)
    out = lax.dot_general(a.astype(jnp.bfloat16), parts, dims, preferred_element_type=F32)
    width = b.shape[1]
    return out[:, :width] + (out[:, width : 2 * width] + out[:, 2 * width :])


def count_dot(a, b):
    return jnp.dot(a.astype(jnp.bfloat16), b.astype(jnp.bfloat16), preferred_element_type=F32)


def iota(shape, dim):
    return lax.broadcasted_iota(jnp.int32, shape, dim).astype(F32)


def as_float(flags):
    return jnp.where(flags, 1.0, 0.0).astype(F32)


def earlier(size):
    return as_float(iota((size, size), 0) < iota((size, size), 1))


def second_onehot(ids_row, count_first, count_second):
    slots = ids_row.shape[1]
    return as_float(ids_row - float(count_first) == iota((count_second, slots), 0))


def fetch_blocks(source, target, sems):
    copies = [
        pltpu.make_async_copy(source.at[pl.ds(k, CHUNK)], target.at[pl.ds(k, CHUNK)], sems.at[k // CHUNK])
        for k in range(0, target.shape[0], CHUNK)
    ]
    for copy in copies:
        copy.start()

    def wait(n):
        if n % CHUNK == 0:
            copies[n // CHUNK].wait()

    return wait


def adjoint_products(kept, rows, spread, parts):
    slots, tile, _ = kept.shape
    for n in range(slots):
        row = rows[0, n]
        total = None
        for i in range(tile // 16):
            part = pl.ds(i * 16, 16)
            term = kept[n, part, :].astype(F32) * spread[row, part, :]
            total = term if total is None else total + term
        parts[n] = total[:8] + total[8:]
    return jnp.sum(parts[...], axis=1)


def spread_duals(dual_t, spread):
    tile = spread.shape[1]
    for r in range(spread.shape[0]):
        spread[r] = jnp.broadcast_to(dual_t[:, r : r + 1], (tile, tile))


def start_kernel(sizes, blocks_in, rows_in, used, columns, dual, bound, cost2, upper2, second, intensity, carbon,
                 ids_out, prod_out, sec_out, dual_out, bound_out, own_out, sum_out, usable_out,
                 spread, parts, squares, prices, rows, blocks, sems, block_sems):
    tile, own2, count_first, count_second = sizes
    slots = blocks.shape[0]
    local_rows = dual.shape[0]
    places = [sec_out.at[pl.ds(count_second + a * own2, own2), :] for a in range(3)]
    copies = [
        pltpu.make_async_copy(source, target, sems.at[k])
        for k, (source, target) in enumerate([
            (dual, squares.at[0, pl.ds(0, local_rows), :]),
            (bound, squares.at[1, pl.ds(0, local_rows), :]),
            (cost2, places[0]),
            (upper2, places[1]),
            (second, places[2]),
            (intensity.at[carbon[0]], prices),
            (rows_in, rows),
        ])
    ]
    for copy in copies:
        copy.start()
    wait = fetch_blocks(blocks_in, blocks, block_sems)
    row = columns[...].astype(F32)
    ids_out[...] = row
    active = as_float(iota((slots, tile), 0) < used[0, 0].astype(F32))
    eye = as_float(iota((slots, slots), 0) == iota((slots, slots), 1))
    column = jnp.sum(eye * row, axis=1, keepdims=True)
    own = as_float(column == row)
    own_out[...] = own
    again = jnp.max(own * earlier(slots), axis=0, keepdims=True)
    some = jnp.max(own * active[:, :1], axis=0, keepdims=True)
    usable_out[...] = as_float(row < float(count_first)) * (1.0 - again) * some
    for k in range(2):
        squares[k, pl.ds(local_rows, tile - local_rows), :] = jnp.zeros((tile - local_rows, tile), F32)
    for copy in copies:
        copy.wait()
    for k, target in enumerate((dual_out, bound_out)):
        target[...] = jnp.transpose(squares[k])
    spread_duals(dual_out[...], spread)
    for n in range(slots):
        wait(n)
        r = rows[0, n]
        total = None
        for i in range(tile // 8):
            term = blocks[n, pl.ds(i * 8, 8), :] * spread[r, pl.ds(i * 8, 8), :]
            total = term if total is None else total + term
        parts[n] = total
    prod = jnp.sum(parts[...], axis=1) * active
    prod_out[...] = prod
    onehot = second_onehot(row, count_first, count_second)
    sums = exact_dot(jnp.concatenate([own, onehot], axis=0), prod)
    sum_out[...] = sums[:slots]
    sec_out[pl.ds(0, count_second), :] = sums[slots:]
    sec_out[pl.ds(count_second, own2), :] += prices[...]


def plan_kernel(sizes, everyone, ids, usable, total, cost, lower, upper, first,
                send_out, pick_out, square, shared):
    devices, slots, shard, most, keep, me_axes = sizes
    me = lax.axis_index(me_axes).astype(F32)
    base = me * float(shard)
    table = everyone[:, 0, :].astype(F32)
    row = ids[...]
    before = earlier(slots)
    asked = as_float((table >= base) & (table < base + float(shard)))
    rank = count_dot(asked, before)
    slot_number = iota((devices, slots), 1)
    lane = iota((devices, 128), 1)
    id_row = jnp.full((devices, 128), -1.0, F32)
    places = []
    for q in range(most):
        chosen = asked * as_float(rank == float(q))
        has = jnp.sum(chosen, axis=1, keepdims=True)
        place = jnp.sum(chosen * (table - base), axis=1, keepdims=True)
        number = jnp.sum(chosen * slot_number, axis=1, keepdims=True)
        places.append(jnp.where(has > 0.0, place, -1.0))
        id_row = jnp.where(lane == float(q), jnp.where(has > 0.0, number, -1.0), id_row)
    wanted = as_float(jnp.concatenate(places, axis=0) == iota((most * devices, shard), 1))
    for a, source in enumerate((cost, lower, upper, first)):
        answer = exact_dot(wanted, source[...])
        for q in range(most):
            send_out[:, q * 4 + a, :] = answer[q * devices : (q + 1) * devices]
    square[...] = jnp.full_like(square, -5.0)
    square[pl.ds(0, devices), pl.ds(0, slots)] = table
    turned = jnp.transpose(square[...])
    for e in range(devices):
        named = as_float(turned[:slots, e : e + 1] == row)
        shared[pl.ds(e, 1), :] = jnp.max(named, axis=0, keepdims=True) * usable[...]
    both = shared[...] * as_float(iota((devices, slots), 0) != me)
    count = jnp.max(jnp.sum(both, axis=1, keepdims=True), axis=0, keepdims=True)
    id_row = jnp.where(lane == float(most + keep), as_float(count > float(keep)), id_row)
    rank = count_dot(both, before)
    picks = []
    for p in range(keep):
        chosen = both * as_float(rank == float(p))
        has = jnp.sum(chosen, axis=1, keepdims=True)
        name = jnp.sum(chosen * row, axis=1, keepdims=True)
        id_row = jnp.where(lane == float(most + p), jnp.where(has > 0.0, name, -1.0), id_row)
        picks.append(chosen)
    pick = jnp.concatenate(picks, axis=0)
    pick_out[...] = pick
    rows = exact_dot(pick, total[...])
    for p in range(keep):
        send_out[:, most * 4 + p, :] = rows[p * devices : (p + 1) * devices]
    send_out[:, most * 4 + keep, :] = id_row


def side_kernel(sizes, everyone, ids, own, pick, cost, lower, upper, first, blocks_in, used,
                base_out, place_out, reply_out, stack_out, kept_out, scale_out, tops, blocks, block_sems):
    devices, slots, shard, most, me_axes = sizes
    wait = fetch_blocks(blocks_in, blocks, block_sems)
    base = lax.axis_index(me_axes).astype(F32) * float(shard)
    table = everyone[:, 0, :].astype(F32)
    row = ids[...]
    before = earlier(slots)
    asked = as_float((table >= base) & (table < base + float(shard)))
    rank = count_dot(asked, before)
    places = []
    for q in range(most):
        chosen = asked * as_float(rank == float(q))
        has = jnp.sum(chosen, axis=1, keepdims=True)
        place = jnp.sum(chosen * (table - base), axis=1, keepdims=True)
        places.append(jnp.where(has > 0.0, place, -1.0))
    wanted = as_float(jnp.concatenate(places, axis=0) == iota((most * devices, shard), 1))
    below = as_float(iota((most * devices, most * devices), 0) > iota((most * devices, most * devices), 1))
    wanted = wanted * as_float(count_dot(below, wanted) == 0.0)
    place_out[...] = wanted
    touched = exact_dot(wanted, jnp.ones((most * devices, cost.shape[1]), F32), (0, 0))
    x = first[...]
    for _ in range(ITERS):
        x = jnp.clip(x - STEP_PRIMAL * cost[...], lower[...], upper[...])
    base_out[...] = jnp.where(touched > 0.0, 0.0, x)
    owner = iota((devices, slots), 0) * float(shard)
    held = as_float((row >= owner) & (row < owner + float(shard)))
    rank = count_dot(held, before)
    for q in range(most):
        reply_out[pl.ds(q * devices, devices), :] = held * as_float(rank == float(q))
    stack_out[pl.ds(0, slots), :] = own[...]
    stack_out[pl.ds(slots, pick.shape[0]), :] = count_dot(pick[...], own[...])
    tile = blocks.shape[1]
    for n in range(slots):
        wait(n)
        top = None
        for i in range(tile // 8):
            size = jnp.abs(blocks[n, pl.ds(i * 8, 8), :])
            top = size if top is None else jnp.maximum(top, size)
        tops[n] = top
    top = jnp.max(jnp.max(tops[...], axis=1), axis=1, keepdims=True)
    factors = jnp.broadcast_to(jnp.where(top > 1e-30, 32767.0 / jnp.maximum(top, 1e-30), 0.0), (slots, tile))
    active = as_float(iota((slots, tile), 0) < used[0, 0].astype(F32))
    scale_out[...] = jnp.broadcast_to(top, (slots, tile)) * (1.0 / 32767.0) * active
    for n in range(slots):
        factor = jnp.broadcast_to(factors[n : n + 1, :], (16, tile))
        for i in range(tile // 16):
            part = pl.ds(i * 16, 16)
            level = jnp.floor(blocks[n, part, :] * factor + 0.5)
            kept_out[n, part, :] = level.astype(jnp.int32).astype(jnp.int16)


def ahead_kernel(sizes, first_step, *refs):
    count_first, count_second, own2, peers = sizes
    refs = list(refs)
    take = lambda: refs.pop(0)
    ids, sec_own = take(), take()
    sec_in = [take() for _ in peers]
    if not first_step:
        y_in, cost2_in, upper2_in = take(), take(), take()
    if first_step:
        cost2_out, upper2_out = take(), take()
    y_out, bars_out, second_all = take(), take(), take()
    if first_step:
        me2 = lax.axis_index(PAIR)
        for k, source in [(0, sec_own)] + list(zip(peers, sec_in)):
            place = pl.multiple_of(lax.bitwise_xor(me2, k) * own2, own2)
            for a in range(3):
                second_all[a, pl.ds(place, own2), :] = source[pl.ds(count_second + a * own2, own2), :]
        cost2, upper2, y = second_all[0], second_all[1], second_all[2]
        cost2_out[...] = cost2
        upper2_out[...] = upper2
    else:
        y, cost2, upper2 = y_in[...], cost2_in[...], upper2_in[...]
    grad2 = sec_own[pl.ds(0, count_second), :]
    for source in sec_in:
        grad2 = grad2 + source[pl.ds(0, count_second), :]
    y_next = jnp.clip(y - STEP_PRIMAL * (cost2 - grad2), 0.0, upper2)
    y_out[...] = y_next
    bars_out[...] = exact_dot(second_onehot(ids[...], count_first, count_second), 2.0 * y_next - y, (0, 0))


def step_kernel(sizes, first_step, last_step, direct, *refs):
    devices, slots, count_first, count_second, own2, peers, most, keep, cells = sizes
    refs = list(refs)
    take = lambda: refs.pop(0)
    kept, scale, rows_in, ids, dual_t, bound_t = [take() for _ in range(6)]
    row = ids[...]
    if first_step:
        answer = take()
        own_sum = None if direct else take()
        gradient = take() if direct else None
    else:
        x_in, cost_in, lower_in, upper_in, match_in = take(), take(), take(), take(), take()
        if direct:
            gradient = take()
        else:
            own_sum, received = take(), take()
    second_bars = take()
    if not last_step:
        if not direct:
            stack_in = take()
    else:
        reply_in = take()
        squares_in = [take() for _ in range(ITERS - 1)]
    if first_step:
        cost_out, lower_out, upper_out, match_out = [take() for _ in range(4)]
        flag_out = None if direct else take()
    if last_step:
        reply_out, dual_out = take(), take()
    else:
        x_out, dual_out, square_out, sec_out, sum_out = [take() for _ in range(5)]
        send_out = None if direct else take()
    spread, parts = take(), take()
    accs = [take() for _ in range(ACCS)]
    square, rows, row_sems = take(), take(), take()
    row_copy = pltpu.make_async_copy(rows_in, rows, row_sems.at[0])
    row_copy.start()

    if first_step:
        id_row = answer[:, most * 4 + keep, :]
        names = jnp.concatenate([id_row[:, q : q + 1] for q in range(most)], axis=0)
        place = as_float(names == iota((most * devices, slots), 1))
        stacked = jnp.concatenate(
            [jnp.concatenate([answer[:, q * 4 + a, :] for q in range(most)], axis=0) for a in range(4)], axis=1
        )
        got = exact_dot(place, stacked, (0, 0))
        width = got.shape[1] // 4
        cost, lower, upper, x = [got[:, a * width : (a + 1) * width] for a in range(4)]
        cost_out[...] = cost
        lower_out[...] = lower
        upper_out[...] = upper
        names = jnp.concatenate([id_row[:, most + p : most + p + 1] for p in range(keep)], axis=0)
        match = as_float(names == row)
        match_out[...] = match
        if not direct:
            flag_out[0, 0] = jnp.where(jnp.max(id_row[:, most + keep : most + keep + 1]) > 0.5, 1, 0)
            fresh = jnp.concatenate([answer[:, most * 4 + p, :] for p in range(keep)], axis=0)
    else:
        x, cost, lower, upper, match = x_in[...], cost_in[...], lower_in[...], upper_in[...], match_in[...]
        if not direct:
            fresh = jnp.concatenate([received[:, p, :] for p in range(keep)], axis=0)
    if direct:
        grad = gradient[...]
    else:
        grad = own_sum[...] + exact_dot(match, fresh, (0, 0))
    x_next = jnp.clip(x - STEP_PRIMAL * (cost - grad), lower, upper)
    onehot = second_onehot(row, count_first, count_second)
    bars = ((2.0 * x_next - x) + second_bars[...]) * scale[...]
    for acc in accs:
        acc[...] = jnp.zeros_like(acc)
    tile = kept.shape[1]
    row_copy.wait()
    for n in range(slots):
        r = rows[0, n]
        acc = accs[n % ACCS]
        bar = jnp.broadcast_to(bars[n : n + 1, :], (16, tile))
        for i in range(tile // 16):
            part = pl.ds(i * 16, 16)
            acc[r, part, :] += kept[n, part, :].astype(F32) * bar
    local_rows = spread.shape[0]
    duals = dual_t[...]
    bounds = bound_t[...]
    lane = lax.broadcasted_iota(jnp.int32, (tile, tile), 1)
    next_dual = jnp.zeros((tile, tile), F32)
    squares = jnp.zeros((tile, 1), F32)
    for r in range(local_rows):
        total = accs[0][r]
        for acc in accs[1:]:
            total = total + acc[r]
        residual = bounds[:, r : r + 1] - jnp.sum(total, axis=1, keepdims=True)
        squares = squares + residual * residual
        column = jnp.maximum(duals[:, r : r + 1] + STEP_DUAL * residual, 0.0)
        wide = jnp.broadcast_to(column, (tile, tile))
        spread[r] = wide
        next_dual = jnp.where(lane == r, wide, next_dual)
    squares = jnp.broadcast_to(jnp.sum(squares, axis=0, keepdims=True), (1, tile))
    if last_step:
        square[...] = jnp.transpose(next_dual)
        dual_out[...] = square[pl.ds(0, local_rows), :]
        lanes = lax.broadcasted_iota(jnp.int32, (1, tile), 1)
        note = jnp.zeros((1, tile), F32)
        for k, value in enumerate([s[...] for s in squares_in] + [squares]):
            note = jnp.where(lanes == k, value, note)
        reply = exact_dot(reply_in[...], x_next)
        for q in range(most):
            reply_out[:, q, :] = reply[q * devices : (q + 1) * devices]
        reply_out[:, most, :] = jnp.broadcast_to(note, (devices, tile))
    else:
        x_out[...] = x_next
        dual_out[...] = next_dual
        square_out[...] = squares
        prod = adjoint_products(kept, rows, spread, parts) * scale[...]
        if direct:
            sec_out[...] = exact_dot(onehot, prod)
            sum_out[...] = prod
        else:
            out = exact_dot(jnp.concatenate([stack_in[...], onehot], axis=0), prod)
            sum_out[...] = out[:slots]
            for p in range(keep):
                send_out[:, p, :] = out[slots + p * devices : slots + (p + 1) * devices]
            sec_out[...] = out[slots + keep * devices :]


def finish_kernel(sizes, reply, base, place, y, dual, first_out, second_out, dual_out, norm_out):
    devices, most, cells, own2 = sizes
    second_out[0] = y[pl.ds(pl.multiple_of(lax.axis_index(PAIR) * own2, own2), own2), :]
    dual_out[0] = dual[...]
    rows = jnp.concatenate([reply[:, q, :] for q in range(most)], axis=0)
    first_out[...] = base[...] + exact_dot(place[...], rows, (0, 0))
    norms = jnp.sqrt(jnp.sum(reply[:, most, :], axis=0, keepdims=True) / float(cells))
    lane = lax.broadcasted_iota(jnp.int32, norms.shape, 1)
    for k in range(ITERS):
        norm_out[k] = jnp.max(jnp.where(lane == k, norms, 0.0))


def shards(
    block_matrices,
    slot_row_block,
    tile_column,
    block_count,
    carbon_scenario,
    intensity,
    cost_first,
    lower_first,
    upper_first,
    cost_second,
    upper_second,
    row_bound,
    first_start,
    second_start,
    dual_start,
):
    devices = lax.axis_size(GROUP)
    pairs = lax.axis_size(PAIR)
    scenarios, slots = slot_row_block.shape
    local_rows, tile = row_bound.shape[1:]
    shard = cost_first.shape[0]
    own2 = cost_second.shape[1]
    count_first = shard * devices
    count_second = own2 * pairs
    cells = scenarios * local_rows * tile * devices
    most = -(-scenarios * slots // devices)
    keep = SHARED
    peers = list(range(1, pairs))

    def shape(*dims):
        return jax.ShapeDtypeStruct(dims, F32)

    def scratch(*dims):
        return pltpu.VMEM(dims, F32)

    params = pltpu.CompilerParams(vmem_limit_bytes=16 << 20)

    def call(kernel, outs, specs, name, *args, scratches=(), out_specs=None):
        return pl.pallas_call(
            kernel,
            out_shape=tuple(outs),
            in_specs=specs,
            out_specs=tuple(out_specs or [VM] * len(outs)),
            scratch_shapes=list(scratches),
            compiler_params=params,
            name=name,
        )(*args)

    def far(value):
        return pltpu.with_memory_space_constraint(value, pltpu.HBM)

    def near(value):
        return pltpu.with_memory_space_constraint(value, pltpu.VMEM)

    block_scratch = [scratch(slots, tile, tile), pltpu.SemaphoreType.DMA((slots // CHUNK,))]
    blocks = far(block_matrices[0])
    everyone = lax.all_to_all(
        jnp.broadcast_to(tile_column[None], (devices, 1, slots)), GROUP, 0, 0, tiled=True
    )
    ids, prod, sec, dual_t, bound_t, own, own_sum, usable = call(
        functools.partial(start_kernel, (tile, own2, count_first, count_second)),
        [shape(1, slots), shape(slots, tile), shape(count_second + 3 * own2, tile), shape(tile, tile),
         shape(tile, tile), shape(slots, slots), shape(slots, tile), shape(1, slots)],
        [HB, HB, SM, VM] + [HB] * 6 + [SM],
        "start",
        blocks, slot_row_block, block_count, tile_column, far(dual_start[0]), far(row_bound[0]), far(cost_second[0]),
        far(upper_second[0]), far(second_start[0]), far(intensity), carbon_scenario,
        scratches=[scratch(local_rows, tile, tile), scratch(slots, 8, tile), scratch(2, tile, tile),
                   scratch(own2, tile), pltpu.SMEM((1, slots), jnp.int32), block_scratch[0], pltpu.SemaphoreType.DMA((7,)), block_scratch[1]],
    )
    firsts = (cost_first, lower_first, upper_first, first_start)
    width = -(-(most * 4 + keep + 1) // 8) * 8
    send, pick = call(
        functools.partial(plan_kernel, (devices, slots, shard, most, keep, GROUP)),
        [shape(devices, width, tile), shape(keep * devices, slots)],
        [VM] * 8,
        "plan",
        everyone, ids, usable, own_sum, *firsts,
        scratches=[scratch(128, 128), scratch(devices, slots)],
    )
    answer = lax.all_to_all(send, GROUP, 0, 0, tiled=True)
    base, place, reply_pick, stack, kept, scale = call(
        functools.partial(side_kernel, (devices, slots, shard, most, GROUP)),
        [shape(shard, tile), shape(most * devices, shard), shape(most * devices, slots),
         shape(slots + keep * devices, slots), pltpu.VMEM((slots, tile, tile), jnp.int16), shape(slots, tile)],
        [VM] * 8 + [HB, SM],
        "side",
        everyone, ids, own, pick, *firsts, blocks, block_count,
        scratches=[scratch(slots, 8, tile)] + block_scratch,
    )

    def swap(value):
        return [lax.ppermute(value, PAIR, [(i, i ^ k) for i in range(pairs)]) for k in peers]

    sec_in = swap(sec)
    step_sizes = (devices, slots, count_first, count_second, own2, peers, most, keep, cells)
    step_scratch = (
        [scratch(local_rows, tile, tile), scratch(slots, 8, tile)]
        + [scratch(local_rows, tile, tile)] * ACCS
        + [scratch(tile, tile), pltpu.SMEM((1, slots), jnp.int32), pltpu.SemaphoreType.DMA((1,))]
    )
    reply_width = -(-(most + 1) // 8) * 8

    def exchange(value):
        gathered = lax.all_gather(value, GROUP, axis=0, tiled=True)
        match = (everyone.astype(F32).reshape(1, -1) == ids.reshape(-1, 1)).astype(F32)
        return jnp.dot(match, gathered, precision=lax.Precision.HIGHEST)

    def run_step(step, direct, args):
        first_step, last_step = step == 0, step == ITERS - 1
        if last_step:
            outs = [shape(devices, reply_width, tile), shape(local_rows, tile)]
        else:
            outs = [shape(slots, tile), shape(tile, tile), shape(1, tile),
                    shape(count_second, tile), shape(slots, tile)]
            if not direct:
                outs.append(shape(devices, keep, tile))
        specs = [VM] * len(outs)
        if first_step:
            lead = [shape(slots, tile)] * 3 + [shape(keep * devices, slots)]
            lead_specs = [VM] * 4
            if not direct:
                lead.append(jax.ShapeDtypeStruct((1, 1), jnp.int32))
                lead_specs.append(SM)
            outs, specs = lead + outs, lead_specs + specs
        return list(call(
            functools.partial(step_kernel, step_sizes, first_step, last_step, direct),
            outs,
            [VM, VM, HB] + [VM] * (len(args) - 3),
            "step",
            *args,
            scratches=step_scratch,
            out_specs=specs,
        ))

    def ahead(step, args):
        first_step = step == 0
        whole = shape(count_second, tile)
        outs = [whole, whole] if first_step else []
        outs += [whole, shape(slots, tile)]
        return call(
            functools.partial(ahead_kernel, (count_first, count_second, own2, peers), first_step),
            outs,
            [VM] * len(args),
            "ahead",
            *args,
            scratches=[scratch(3, count_second, tile)],
        )

    def begin(direct, answer, own_sum, dual_t, second_bars):
        args = [near(kept), scale, slot_row_block, ids, dual_t, bound_t, answer, own_sum, second_bars]
        if not direct:
            args.append(stack)
        return run_step(0, direct, args)

    def proceed(direct, fixed, state, second):
        squares = []
        cost, lower, upper, match = fixed
        cost2, upper2, y = second
        for step in range(1, ITERS):
            x, dual_t, square, sec, own_sum = state[:5]
            squares.append(square)
            y, second_bars = ahead(step, [ids, sec] + swap(sec) + [y, cost2, upper2])
            args = [near(kept), scale, slot_row_block, ids, dual_t, bound_t, x, cost, lower, upper, match]
            if direct:
                args.append(exchange(own_sum))
            else:
                args += [own_sum, lax.all_to_all(state[5], GROUP, 0, 0, tiled=True)]
            args.append(second_bars)
            if step == ITERS - 1:
                args += [reply_pick] + squares
            elif not direct:
                args.append(stack)
            state = run_step(step, direct, args)
        reply, dual = state
        return lax.all_to_all(reply, GROUP, 0, 0, tiled=True), y, dual

    cost2, upper2, y, second_bars = ahead(0, [ids, sec] + sec_in)

    def general(operands):
        (answer, prod, dual_t, second_bars), second, _ = operands
        results = begin(True, answer, exchange(prod), dual_t, second_bars)
        return proceed(True, results[:4], results[4:], second)

    def usual(operands):
        _, second, results = operands
        return proceed(False, results[:4], results[5:], second)

    results = begin(False, answer, own_sum, dual_t, second_bars)
    reply, y, dual = lax.cond(
        results[4][0, 0] > 0,
        general,
        usual,
        ((answer, prod, dual_t, second_bars), (cost2, upper2, y), results),
    )
    return call(
        functools.partial(finish_kernel, (devices, most, cells, own2)),
        [shape(shard, tile), shape(1, own2, tile), shape(1, local_rows, tile), shape(ITERS)],
        [VM] * 5,
        "finish",
        reply, base, place, y, dual,
        out_specs=[VM, VM, VM, SM],
    )


def solution(mesh):
    return jax.shard_map(
        shards,
        mesh=mesh,
        in_specs=(
            P(("grp", "scen"), ("blk", "sub"), None, None),
            P(("grp", "scen"), ("blk", "sub")),
            P(("grp", "scen"), ("blk", "sub")),
            P(("grp", "scen"), ("blk", "sub")),
            P(("grp", "scen")),
            P(None, ("blk", "sub"), None),
            P(("grp", "scen", "blk", "sub"), None),
            P(("grp", "scen", "blk", "sub"), None),
            P(("grp", "scen", "blk", "sub"), None),
            P(("grp", "scen"), ("blk", "sub"), None),
            P(("grp", "scen"), ("blk", "sub"), None),
            P(("grp", "scen"), ("blk", "sub"), None),
            P(("grp", "scen", "blk", "sub"), None),
            P(("grp", "scen"), ("blk", "sub"), None),
            P(("grp", "scen"), ("blk", "sub"), None),
        ),
        out_specs=(
            P(("grp", "scen", "blk", "sub"), None),
            P(("grp", "scen"), ("blk", "sub"), None),
            P(("grp", "scen"), ("blk", "sub"), None),
            P("grp"),
        ),
        check_vma=False,
    )
```
